256 devices in a mesh: tm: 8 (over x_hi, y), rows: 32 (over z, x_lo, core).
Axes of the slice: x: 4 (x_hi: 2, x_lo: 2; x = x_hi * 2 + x_lo), y: 4, z: 8, core: 2. Of those that a mesh axis runs over, the one named last changes fastest.
Arguments:
- features: bfloat16 [32, 64, 64, 384], P('tm', 'rows'), may hold values from -6 to 6
- first_weight: bfloat16 [3, 3, 3, 384, 192], replicated, may hold values from -0.0625 to 0.0625
- first_bias: float32 [192], replicated, may hold values from -1.5 to 1.5
- first_gain: float32 [384], replicated, may hold values from 0.25 to 1.75
- second_weight: bfloat16 [3, 3, 3, 192, 192], replicated, may hold values from -0.078125 to 0.078125
- second_bias: float32 [192], replicated, may hold values from -1.5 to 1.5
- second_gain: float32 [192], replicated, may hold values from 0.25 to 1.75
- skip_weight: bfloat16 [384, 192], replicated, may hold values from -0.3125 to 0.3125
- skip_bias: float32 [192], replicated, may hold values from -1.5 to 1.5
Outputs:
- block_out: bfloat16 [32, 64, 64, 192], P('tm', 'rows')
The draws below stay inside these ranges and needn't reach their ends.
All inputs are finite; a program needn't handle non-finite values.
Results may differ from the reference program's by a relative error of at most 0.01.
Values may be sent and summed in bfloat16 or wider, within the bound.
No kernel may reach another device: no remote copies, remote signals or barrier semaphores. Data moves between devices by JAX's collectives and lax.ppermute only.
A program may use at most 64 MiB of HBM per device.

```python
import jax
import jax.numpy as jnp
from jax import lax

C1 = 384
C2 = 192
W = 64
NT = 32
NH = 64


def block_levels(own_key, dims, pieces, least, largest):
    factor_of = 1.0
    for position, parts in pieces:
        steps = jax.random.uniform(jax.random.fold_in(jax.random.fold_in(own_key, 6), position), (parts,), jnp.float32, least / len(pieces), largest / len(pieces))
        factor_of = factor_of * jnp.repeat(jnp.exp(steps), dims[position] // parts).reshape((-1,) + (1,) * (len(dims) - 1 - position))
    return factor_of


def centred(key, dims, width, bound, cuts=(), kind=jnp.bfloat16):
    values = width * jax.random.normal(key, dims, jnp.float32)
    if cuts:
        values = values * block_levels(key, dims, cuts, -0.22, 0.18)
    return jnp.clip(values, -bound, bound).astype(kind)


def setup_inputs(seed: int = 0) -> dict:
    seeds = jax.random.split(jax.random.key(seed), 10)
    features = centred(seeds[0], (NT, NH, W, C1), 1.0, 6.0, ((0, 8), (1, 32)))
    first_weight = centred(seeds[1], (3, 3, 3, C1, C2), (27 * C1) ** -0.5, 0.0625)
    first_bias = centred(seeds[2], (C2,), 0.3, 1.5, (), jnp.float32)
    first_gain = jnp.clip(1.0 + 0.15 * jax.random.normal(seeds[3], (C1,), jnp.float32), 0.25, 1.75)
    second_weight = centred(seeds[4], (3, 3, 3, C2, C2), (27 * C2) ** -0.5, 0.078125)
    second_bias = centred(seeds[5], (C2,), 0.3, 1.5, (), jnp.float32)
    second_gain = jnp.clip(1.0 + 0.15 * jax.random.normal(seeds[6], (C2,), jnp.float32), 0.25, 1.75)
    skip_weight = centred(seeds[7], (C1, C2), C1 ** -0.5, 0.3125)
    skip_bias = centred(seeds[8], (C2,), 0.3, 1.5, (), jnp.float32)
    return {"features": features, "first_weight": first_weight, "first_bias": first_bias, "first_gain": first_gain, "second_weight": second_weight, "second_bias": second_bias, "second_gain": second_gain, "skip_weight": skip_weight, "skip_bias": skip_bias}


def activate(values, gain):
    floats = values.astype(jnp.float32)
    scaled = floats * lax.rsqrt(lax.optimization_barrier(jnp.mean(floats * floats, axis=-1, keepdims=True)) + 1e-06) * gain
    return jax.nn.silu(scaled).astype(jnp.bfloat16)

def convolve(padded, weight, bias):
    frames = padded.shape[0] - 2
    height = padded.shape[1] - 2
    across = padded.shape[2]
    channels = padded.shape[3]
    outputs = weight.shape[4]
    widened = jnp.pad(padded, ((0, 0), (0, 0), (1, 1), (0, 0)))
    summed = jnp.zeros((frames * height * across, outputs), jnp.float32)
    for time_tap in range(3):
        for row_tap in range(3):
            stacked = jnp.concatenate([widened[time_tap:time_tap + frames, row_tap:row_tap + height, col_tap:col_tap + across] for col_tap in range(3)], axis=-1)
            summed = summed + jnp.dot(stacked.reshape(-1, 3 * channels), weight[time_tap, row_tap].reshape(3 * channels, outputs), preferred_element_type=jnp.float32)
    return summed.reshape(frames, height, across, outputs) + bias

def reference(features, first_weight, first_bias, first_gain, second_weight, second_bias, second_gain, skip_weight, skip_bias):
    first_act = activate(features, first_gain)
    padded = jnp.pad(first_act, ((2, 0), (1, 1), (0, 0), (0, 0)))
    hidden = convolve(padded, first_weight, first_bias).astype(jnp.bfloat16)
    second_act = activate(hidden, second_gain)
    padded = jnp.pad(second_act, ((2, 0), (1, 1), (0, 0), (0, 0)))
    branch = convolve(padded, second_weight, second_bias)
    skipped = jnp.dot(features.reshape(-1, features.shape[-1]), skip_weight, preferred_element_type=jnp.float32)
    skipped = skipped.reshape(branch.shape)
    return (branch + skipped + skip_bias).astype(jnp.bfloat16)
```

```python
import jax
import jax.numpy as jnp
from jax import lax
from jax.experimental import pallas as pl
from jax.experimental.pallas import tpu as pltpu
from jax.sharding import PartitionSpec as P

F32 = jnp.float32
BF16 = jnp.bfloat16
COLS = 64
VMEM = pl.BlockSpec(memory_space=pltpu.VMEM)


def call(body, outs, *args, flops=0, scratch=(), limit=8):
    moved = sum(a.size * a.dtype.itemsize for a in args) + sum(o.size * o.dtype.itemsize for o in outs)
    return pl.pallas_call(
        body,
        out_shape=outs,
        in_specs=[VMEM] * len(args),
        out_specs=[VMEM] * len(outs),
        scratch_shapes=list(scratch),
        compiler_params=pltpu.CompilerParams(vmem_limit_bytes=limit << 20),
        cost_estimate=pl.CostEstimate(flops=flops, bytes_accessed=moved, transcendentals=0),
    )(*args)


def act(values, gain):
    mean = jnp.mean(values * values, axis=-1, keepdims=True)
    scaled = values * lax.rsqrt(mean + 1e-06) * gain
    return scaled / (1.0 + jnp.exp(-scaled))


def taps(values):
    count = values.shape[0]
    col = lax.broadcasted_iota(jnp.int32, values.shape, 0) % COLS
    left = jnp.where(col == 0, 0.0, pltpu.roll(values, 1, 0))
    right = jnp.where(col == COLS - 1, 0.0, pltpu.roll(values, count - 1, 0))
    return left, values, right


def dot_nt(a, w):
    return lax.dot_general(a, w, (((1,), (1,)), ((), ())), preferred_element_type=F32)


def dot_nn(a, w):
    return jnp.dot(a, w, preferred_element_type=F32)


def act_kernel(x_ref, g_ref, fa_ref, a_ref, b_ref):
    odd = lax.axis_index("rows") % 2
    gain = g_ref[...]
    for row in range(2):
        for t in range(4):
            values = act(x_ref[t, row].astype(F32), gain)
            left, mid, right = taps(values)
            mid = mid.astype(BF16)
            fa_ref[row, t, :, 0:384] = left.astype(BF16)
            fa_ref[row, t, :, 384:768] = mid
            fa_ref[row, t, :, 768:1152] = right.astype(BF16)

            @pl.when(odd == row)
            def _():
                b_ref[t] = mid

            @pl.when(odd != row)
            def _():
                a_ref[t] = mid


def first_own_kernel(fa_ref, w_ref, acc_ref):
    acc_ref[...] = jnp.zeros_like(acc_ref)
    for i in range(3):
        for j in (1, 0, 2):
            w = jnp.concatenate([w_ref[i, j, k] for k in range(3)], axis=-1)
            if j == 1:
                out = dot_nt(fa_ref[...].reshape(512, 1152), w).reshape(2, 4, COLS, 192)
                acc_ref[:, 2 - i : 6 - i] += out
            else:
                source = 0 if j == 0 else 1
                out = dot_nt(fa_ref[source].reshape(256, 1152), w).reshape(4, COLS, 192)
                acc_ref[1 - source, 2 - i : 6 - i] += out


def rims(ra_ref, rb_ref):
    rows = lax.axis_index("rows")
    odd = rows % 2 == 1
    count = lax.axis_size("rows")
    a = ra_ref[...].astype(F32)
    edge = jnp.logical_or(rows == 0, rows == count - 1)
    b = jnp.where(edge, 0.0, rb_ref[...].astype(F32))
    return jnp.where(odd, a, b), jnp.where(odd, b, a)


def first_rim_kernel(own_ref, ra_ref, rb_ref, w_ref, bias_ref, gain_ref, p_ref, s_ref, t_ref, acc_ref):
    acc_ref[...] = own_ref[...]
    for row, rim in enumerate(rims(ra_ref, rb_ref)):
        stacked = jnp.concatenate([v.astype(BF16) for v in taps(rim.reshape(256, 384))], axis=-1)
        for i in range(3):
            w = jnp.concatenate([w_ref[i, 2 * row, k] for k in range(3)], axis=-1)
            acc_ref[row, 2 - i : 6 - i] += dot_nt(stacked, w).reshape(4, COLS, 192)
    p_ref[...] = acc_ref[:, 0:2]
    hidden = (acc_ref[:, 2:4] + bias_ref[...]).astype(BF16).astype(F32)
    second = act(hidden, gain_ref[...])
    s_ref[...] = second.astype(BF16)
    t_ref[...] = jnp.concatenate([acc_ref[:, 4:6], second], axis=-1).astype(BF16)


def second_act_kernel(p_ref, t_ref, s_ref, bias_ref, gain_ref, sa_ref, a_ref, b_ref):
    first = lax.axis_index("tm") == 0
    odd = lax.axis_index("rows") % 2
    came = jnp.where(first, 0.0, t_ref[...].astype(F32))
    hidden = (p_ref[...] + came[..., :192] + bias_ref[...]).astype(BF16).astype(F32)
    second = act(hidden, gain_ref[...])
    for row in range(2):
        frames = jnp.concatenate([came[row, :, :, 192:], second[row], s_ref[row].astype(F32)], axis=0)
        left, mid, right = taps(frames.reshape(384, 192))
        stacked = jnp.concatenate([left, mid, right], axis=-1).astype(BF16)
        sa_ref[row] = stacked.reshape(6, COLS, 576)
        packed = jnp.concatenate([frames[0:3], frames[3:6]], axis=-1).astype(BF16)

        @pl.when(odd == row)
        def _():
            b_ref[...] = packed

        @pl.when(odd != row)
        def _():
            a_ref[...] = packed


def second_own_kernel(sa_ref, w_ref, x_ref, sw_ref, bias_ref, sbias_ref, acc_ref):
    bias = bias_ref[...] + sbias_ref[...]
    for row in range(2):
        acc_ref[row] = dot_nt(x_ref[:, row].reshape(256, 384), sw_ref[...]).reshape(4, COLS, 192) + bias
    for i in range(3):
        for j in (1, 0, 2):
            w = w_ref[i, j].reshape(576, 192)
            if j == 1:
                out = dot_nn(sa_ref[:, i : i + 4].reshape(512, 576), w).reshape(2, 4, COLS, 192)
                acc_ref[...] += out
            else:
                source = 0 if j == 0 else 1
                out = dot_nn(sa_ref[source, i : i + 4].reshape(256, 576), w)
                acc_ref[1 - source] += out.reshape(4, COLS, 192)


def second_rim_kernel(acc_ref, ra_ref, rb_ref, w_ref, out_ref):
    for row, rim in enumerate(rims(ra_ref, rb_ref)):
        frames = jnp.concatenate([rim[..., :192], rim[..., 192:]], axis=0)
        left, mid, right = taps(frames.reshape(384, 192))
        stacked = jnp.concatenate([left, mid, right], axis=-1).astype(BF16).reshape(6, COLS, 576)
        total = acc_ref[row]
        for i in range(3):
            w = w_ref[i, 2 * row].reshape(576, 192)
            total += dot_nn(stacked[i : i + 4].reshape(256, 576), w).reshape(4, COLS, 192)
        out_ref[:, row] = total.astype(BF16)


def swap_pairs(count):
    inner = [(i, i ^ 1) for i in range(count)]
    outer = [(0, 0), (count - 1, count - 1)]
    for i in range(1, count - 1, 2):
        outer += [(i, i + 1), (i + 1, i)]
    return inner, outer


def shape(dims, dtype):
    return jax.ShapeDtypeStruct(dims, dtype)


def per_device(x, w1, b1, g1, w2, b2, g2, sw, sb):
    inner, outer = swap_pairs(lax.axis_size("rows"))
    steps = lax.axis_size("tm")
    ring = [(i, (i + 1) % steps) for i in range(steps)]
    w1 = jnp.swapaxes(w1, 3, 4)
    sw = jnp.swapaxes(sw, 0, 1)
    b1, g1, b2, g2, sb = (v.reshape(1, -1) for v in (b1, g1, b2, g2, sb))

    fa, send_a, send_b = call(
        act_kernel,
        [shape((2, 4, COLS, 1152), BF16), shape((4, COLS, 384), BF16), shape((4, COLS, 384), BF16)],
        x, g1,
    )
    rim_b = lax.ppermute(send_b, "rows", outer)
    rim_a = lax.ppermute(send_a, "rows", inner)
    acc = call(first_own_kernel, [shape((2, 6, COLS, 192), F32)], fa, w1, flops=10**9)[0]
    p01, s23, send_t = call(
        first_rim_kernel,
        [shape((2, 2, COLS, 192), F32), shape((2, 2, COLS, 192), BF16), shape((2, 2, COLS, 384), BF16)],
        acc, rim_a, rim_b, w1, b1, g2, flops=10**9, scratch=[pltpu.VMEM((2, 6, COLS, 192), F32)],
    )
    came = lax.ppermute(send_t, "tm", ring)
    sa, send_a, send_b = call(
        second_act_kernel,
        [shape((2, 6, COLS, 576), BF16), shape((3, COLS, 384), BF16), shape((3, COLS, 384), BF16)],
        p01, came, s23, b1, g2,
    )
    rim_b = lax.ppermute(send_b, "rows", outer)
    rim_a = lax.ppermute(send_a, "rows", inner)
    acc = call(second_own_kernel, [shape((2, 4, COLS, 192), F32)], sa, w2, x, sw, b2, sb, flops=10**9)[0]
    return call(second_rim_kernel, [shape((4, 2, COLS, 192), BF16)], acc, rim_a, rim_b, w2, flops=10**9)[0]


def solution(mesh):
    return jax.shard_map(
        per_device,
        mesh=mesh,
        in_specs=(P("tm", "rows", None, None), P(), P(), P(), P(), P(), P(), P(), P()),
        out_specs=P("tm", "rows", None, None),
        check_vma=False,
    )
```

```python
import jax
import jax.numpy as jnp
from jax import lax
from jax.experimental import pallas as pl
from jax.experimental.pallas import tpu as pltpu
from jax.sharding import PartitionSpec as P

F32 = jnp.float32
BF16 = jnp.bfloat16
COLS = 64
VMEM = pl.BlockSpec(memory_space=pltpu.VMEM)
HBM = pl.BlockSpec(memory_space=pltpu.HBM)


def call(body, outs, *args, flops=0, scratch=(), limit=8, in_hbm=(), out_hbm=()):
    args = [pltpu.with_memory_space_constraint(a, pltpu.HBM) if n in in_hbm else a for n, a in enumerate(args)]
    moved = sum(a.size * a.dtype.itemsize for a in args) + sum(o.size * o.dtype.itemsize for o in outs)
    return pl.pallas_call(
        body,
        out_shape=outs,
        in_specs=[HBM if n in in_hbm else VMEM for n in range(len(args))],
        out_specs=[HBM if n in out_hbm else VMEM for n in range(len(outs))],
        scratch_shapes=list(scratch),
        compiler_params=pltpu.CompilerParams(vmem_limit_bytes=limit << 20),
        cost_estimate=pl.CostEstimate(flops=flops, bytes_accessed=moved, transcendentals=0),
    )(*args)


def shape(dims, dtype=BF16):
    return jax.ShapeDtypeStruct(dims, dtype)


def act(values, gain):
    mean = jnp.mean(values * values, axis=-1, keepdims=True)
    scaled = values * lax.rsqrt(mean + 1e-06) * gain
    return scaled / (1.0 + jnp.exp(-scaled))


def taps(values):
    count = values.shape[0]
    col = lax.broadcasted_iota(jnp.int32, values.shape, 0) % COLS
    left = jnp.where(col == 0, 0.0, pltpu.roll(values, 1, 0))
    right = jnp.where(col == COLS - 1, 0.0, pltpu.roll(values, count - 1, 0))
    return left, values, right


def first_dot(a, w_ref, i, j):
    frames = a.shape[0]
    w = jnp.concatenate([w_ref[i, j, k] for k in range(3)], axis=-1)
    out = lax.dot_general(
        a.reshape(frames * COLS, 1152), w, (((1,), (1,)), ((), ())), preferred_element_type=F32
    )
    return out.reshape(frames, COLS, 192)


def second_dot(a, w_ref, i, j):
    frames = a.shape[0]
    out = jnp.dot(a.reshape(frames * COLS, 576), w_ref[i, j].reshape(576, 192), preferred_element_type=F32)
    return out.reshape(frames, COLS, 192)


def store_for_pairs(above, below, a_ref, b_ref):
    odd = lax.axis_index("rows") % 2 == 1
    a_ref[...] = jnp.where(odd, above, below).astype(BF16)
    b_ref[...] = jnp.where(odd, below, above).astype(BF16)


def from_pairs(ra_ref, rb_ref):
    rows = lax.axis_index("rows")
    odd = rows % 2 == 1
    edge = jnp.logical_or(rows == 0, rows == lax.axis_size("rows") - 1)
    a = ra_ref[...].astype(F32)
    b = jnp.where(edge, 0.0, rb_ref[...].astype(F32))
    return jnp.where(odd, a, b), jnp.where(odd, b, a)


def pack(values):
    half = values.shape[0] // 2
    return jnp.concatenate([values[:half], values[half:]], axis=-1)


def unpack(values):
    return jnp.concatenate([values[..., :192], values[..., 192:]], axis=0)


def act_kernel(x_hbm, g_hbm, w_hbm, fa_ref, w_ref, a_ref, b_ref, x_ref, g_ref, acc_ref, gsem, xsem, wsem):
    gain_load = pltpu.make_async_copy(g_hbm, g_ref, gsem)
    gain_load.start()
    loads = [pltpu.make_async_copy(x_hbm.at[t], x_ref.at[t], xsem.at[t]) for t in range(4)]
    weights = [pltpu.make_async_copy(w_hbm.at[:, j], w_ref.at[:, j], wsem.at[j]) for j in range(3)]
    for load in loads:
        load.start()
    for j in (0, 2, 1):
        weights[j].start()
    gain_load.wait()
    gain = g_ref[...].reshape(1, 384)
    for t in range(4):
        loads[t].wait()
        for row in range(2):
            left, mid, right = taps(act(x_ref[t, row].astype(F32), gain))
            fa_ref[row, t, :, 0:384] = left.astype(BF16)
            fa_ref[row, t, :, 384:768] = mid.astype(BF16)
            fa_ref[row, t, :, 768:1152] = right.astype(BF16)
    weights[0].wait()
    weights[2].wait()
    sums = []
    for side, j in ((0, 2), (1, 0)):
        acc_ref[side, 2:6] = first_dot(fa_ref[side], w_ref, 0, j)
        acc_ref[side, 0:2] = jnp.zeros((2, COLS, 192), F32)
        for i in (1, 2):
            acc_ref[side, 2 - i : 6 - i] += first_dot(fa_ref[side], w_ref, i, j)
        sums.append(pack(acc_ref[side]))
    store_for_pairs(sums[0], sums[1], a_ref, b_ref)
    weights[1].wait()


def first_own_kernel(fa_ref, w_ref, acc_ref):
    for i in range(3):
        outs = [first_dot(fa_ref[row], w_ref, i, 1) for row in range(2)]
        outs[1] += first_dot(fa_ref[0], w_ref, i, 0)
        outs[0] += first_dot(fa_ref[1], w_ref, i, 2)
        for row in range(2):
            if i == 0:
                acc_ref[row, 0:2] = jnp.zeros((2, COLS, 192), F32)
                acc_ref[row, 2:6] = outs[row]
            else:
                acc_ref[row, 2 - i : 6 - i] += outs[row]


def first_rim_kernel(own_ref, ra_ref, rb_ref, bias_ref, gain_ref, p_ref, s_ref, t_ref):
    for row, rim in enumerate(from_pairs(ra_ref, rb_ref)):
        total = own_ref[row] + unpack(rim)
        p_ref[row] = total[0:2] + bias_ref[...]
        hidden = (total[2:4] + bias_ref[...]).astype(BF16).astype(F32)
        second = act(hidden, gain_ref[...])
        s_ref[row] = second.astype(BF16)
        t_ref[row] = jnp.concatenate([total[4:6], second], axis=-1).astype(BF16)


def meanwhile_kernel(s_ref, x_ref, w_ref, bias_ref, sbias_ref, sa_ref, acc_ref):
    bias = bias_ref[...] + sbias_ref[...]
    for row in range(2):
        stacked = jnp.concatenate(taps(s_ref[row].astype(F32).reshape(128, 192)), axis=-1)
        sa_ref[row] = stacked.astype(BF16).reshape(2, COLS, 576)
        out = lax.dot_general(
            x_ref[:, row].reshape(256, 384), w_ref[...], (((1,), (1,)), ((), ())), preferred_element_type=F32
        )
        acc_ref[row] = out.reshape(4, COLS, 192) + bias


def second_act_kernel(p_ref, t_ref, last_ref, gain_ref, w_ref, sa_ref, a_ref, b_ref):
    first = lax.axis_index("tm") == 0
    for row in range(2):
        came = jnp.where(first, 0.0, t_ref[row].astype(F32))
        hidden = (p_ref[row] + came[..., :192]).astype(BF16).astype(F32)
        second = act(hidden, gain_ref[...])
        frames = jnp.concatenate([came[..., 192:], second], axis=0)
        stacked = jnp.concatenate(taps(frames.reshape(256, 192)), axis=-1)
        sa_ref[row, 0:4] = stacked.astype(BF16).reshape(4, COLS, 576)
        sa_ref[row, 4:6] = last_ref[row]
    sums = []
    for side, j in ((0, 2), (1, 0)):
        total = second_dot(sa_ref[side, 0:4], w_ref, 0, j)
        total += second_dot(sa_ref[side, 1:5], w_ref, 1, j)
        total += second_dot(sa_ref[side, 2:6], w_ref, 2, j)
        sums.append(pack(total))
    store_for_pairs(sums[0], sums[1], a_ref, b_ref)


def second_own_kernel(sa_ref, w_ref, skip_ref, acc_ref):
    for i in range(3):
        outs = [second_dot(sa_ref[row, i : i + 4], w_ref, i, 1) for row in range(2)]
        outs[1] += second_dot(sa_ref[0, i : i + 4], w_ref, i, 0)
        outs[0] += second_dot(sa_ref[1, i : i + 4], w_ref, i, 2)
        for row in range(2):
            if i == 0:
                acc_ref[row] = skip_ref[row] + outs[row]
            else:
                acc_ref[row] += outs[row]


def second_rim_kernel(acc_ref, ra_ref, rb_ref, out_ref):
    for row, rim in enumerate(from_pairs(ra_ref, rb_ref)):
        out_ref[:, row] = (acc_ref[row] + unpack(rim)).astype(BF16)


def swap_pairs(count):
    inner = [(i, i ^ 1) for i in range(count)]
    outer = [(0, 0), (count - 1, count - 1)]
    for i in range(1, count - 1, 2):
        outer += [(i, i + 1), (i + 1, i)]
    return inner, outer


def per_device(x, w1, b1, g1, w2, b2, g2, sw, sb):
    inner, outer = swap_pairs(lax.axis_size("rows"))
    steps = lax.axis_size("tm")
    ring = [(i, (i + 1) % steps) for i in range(steps)]
    w1 = jnp.swapaxes(w1, 3, 4)
    sw = jnp.swapaxes(sw, 0, 1)
    b1, b2, g2, sb = (v.reshape(1, -1) for v in (b1, b2, g2, sb))

    def swap(a, b):
        return lax.ppermute(a, "rows", inner), lax.ppermute(b, "rows", outer)

    fa, w1, send_a, send_b = call(
        act_kernel,
        [shape((2, 4, COLS, 1152)), shape(w1.shape), shape((3, COLS, 384)), shape((3, COLS, 384))],
        x, g1, w1, flops=10**9, in_hbm=(0, 1, 2),
        scratch=[
            pltpu.VMEM((4, 2, COLS, 384), BF16), pltpu.VMEM((384,), F32), pltpu.VMEM((2, 6, COLS, 192), F32),
            pltpu.SemaphoreType.DMA(()), pltpu.SemaphoreType.DMA((4,)), pltpu.SemaphoreType.DMA((3,)),
        ],
    )
    rims = swap(send_a, send_b)
    own = call(first_own_kernel, [shape((2, 6, COLS, 192), F32)], fa, w1, flops=10**9)[0]
    p01, s23, send_t = call(
        first_rim_kernel,
        [shape((2, 2, COLS, 192), F32), shape((2, 2, COLS, 192)), shape((2, 2, COLS, 384))],
        own, *rims, b1, g2, flops=10**8,
    )
    came = lax.ppermute(send_t, "tm", ring)
    last, skip = call(
        meanwhile_kernel,
        [shape((2, 2, COLS, 576)), shape((2, 4, COLS, 192), F32)],
        s23, x, sw, b2, sb, flops=10**8,
    )
    sa, send_a, send_b = call(
        second_act_kernel,
        [shape((2, 6, COLS, 576)), shape((2, COLS, 384)), shape((2, COLS, 384))],
        p01, came, last, g2, w2, flops=10**9,
    )
    rims = swap(send_a, send_b)
    own = call(second_own_kernel, [shape((2, 4, COLS, 192), F32)], sa, w2, skip, flops=10**9)[0]
    return call(second_rim_kernel, [shape((4, 2, COLS, 192))], own, *rims, flops=10**8)[0]


def solution(mesh):
    return jax.shard_map(
        per_device,
        mesh=mesh,
        in_specs=(P("tm", "rows", None, None), P(), P(), P(), P(), P(), P(), P(), P()),
        out_specs=P("tm", "rows", None, None),
        check_vma=False,
    )
```

```python
import jax
import jax.numpy as jnp
from jax import lax
from jax.experimental import pallas as pl
from jax.experimental.pallas import tpu as pltpu
from jax.sharding import PartitionSpec as P

F32 = jnp.float32
BF16 = jnp.bfloat16
COLS = 64
VMEM = pl.BlockSpec(memory_space=pltpu.VMEM)
HBM = pl.BlockSpec(memory_space=pltpu.HBM)


def call(body, outs, *args, flops=0, scratch=(), limit=8, in_hbm=()):
    args = [pltpu.with_memory_space_constraint(a, pltpu.HBM) if n in in_hbm else a for n, a in enumerate(args)]
    moved = sum(a.size * a.dtype.itemsize for a in args) + sum(o.size * o.dtype.itemsize for o in outs)
    return pl.pallas_call(
        body,
        out_shape=outs,
        in_specs=[HBM if n in in_hbm else VMEM for n in range(len(args))],
        out_specs=[VMEM] * len(outs),
        scratch_shapes=list(scratch),
        compiler_params=pltpu.CompilerParams(vmem_limit_bytes=limit << 20),
        cost_estimate=pl.CostEstimate(flops=flops, bytes_accessed=moved, transcendentals=0),
    )(*args)


def shape(dims, dtype=BF16):
    return jax.ShapeDtypeStruct(dims, dtype)


def act(values, gain):
    mean = jnp.mean(values * values, axis=-1, keepdims=True)
    scaled = values * lax.rsqrt(mean + 1e-06) * gain
    return scaled / (1.0 + jnp.exp(-scaled))


def taps(values):
    frames, _, channels = values.shape
    flat = values.reshape(frames * COLS, channels)
    col = lax.broadcasted_iota(jnp.int32, flat.shape, 0) % COLS
    left = jnp.where(col == 0, 0.0, pltpu.roll(flat, 1, 0))
    right = jnp.where(col == COLS - 1, 0.0, pltpu.roll(flat, frames * COLS - 1, 0))
    return jnp.concatenate([left, flat, right], axis=-1).astype(BF16).reshape(frames, COLS, 3 * channels)


def first_sums(fa_ref, w_ref, acc_ref):
    acc_ref[...] = jnp.zeros_like(acc_ref)
    for i in range(3):
        a = fa_ref[:, i : i + 2].reshape(4 * COLS, 1152)
        for j in range(3):
            w = jnp.concatenate([w_ref[i, j, k] for k in range(3)], axis=-1)
            out = lax.dot_general(a, w, (((1,), (1,)), ((), ())), preferred_element_type=F32)
            acc_ref[2 - j : 4 - j] += out.reshape(2, 2, COLS, 192)


def send_rows(acc_ref, a_ref, b_ref):
    odd = lax.axis_index("rows") % 2 == 1
    up = jnp.concatenate([acc_ref[0], acc_ref[1]], axis=-1)
    down = jnp.concatenate([acc_ref[2], acc_ref[3]], axis=-1)
    a_ref[...] = jnp.where(odd, up, down).astype(BF16)
    b_ref[...] = jnp.where(odd, down, up).astype(BF16)


def second_act(own_ref, rb_ref, ra_ref, bias_ref, gain_ref, sa_ref):
    rows = lax.axis_index("rows")
    odd = rows % 2 == 1
    a, b = ra_ref[...].astype(F32), rb_ref[...].astype(F32)
    above, below = jnp.where(odd, a, b), jnp.where(odd, b, a)
    top, bottom = rows == 0, rows == lax.axis_size("rows") - 1
    above, below = jnp.where(top, 0.0, above), jnp.where(bottom, 0.0, below)
    for row, rim in enumerate((above[..., :192], above[..., 192:], below[..., :192], below[..., 192:])):
        hidden = (own_ref[row] + rim + bias_ref[...]).astype(BF16).astype(F32)
        second = act(hidden, gain_ref[...])
        if row == 0:
            second = jnp.where(top, 0.0, second)
        if row == 3:
            second = jnp.where(bottom, 0.0, second)
        sa_ref[row] = taps(second)


def second_dot(a, w_ref, i, j):
    rows, frames = a.shape[:2]
    a = a.reshape(rows * frames * COLS, 576)
    out = jnp.dot(a, w_ref[i, j].reshape(576, 192), preferred_element_type=F32)
    return out.reshape(rows, frames, COLS, 192)


def act_kernel(x_hbm, g_hbm, fa_ref, t_ref, x_ref, g_ref, gsem, sem):
    gain_load = pltpu.make_async_copy(g_hbm, g_ref, gsem)
    loads = [pltpu.make_async_copy(x_hbm.at[t], x_ref.at[t], sem.at[t]) for t in range(4)]
    for load in [gain_load] + loads:
        load.start()
    gain_load.wait()
    gain = g_ref[...].reshape(1, 384)
    for t in range(4):
        loads[t].wait()
        for row in range(2):
            value = act(x_ref[t, row].astype(F32), gain)
            fa_ref[row, t] = taps(value[None])[0]
            if t >= 2:
                t_ref[row, t - 2] = value.astype(BF16)


def early_kernel(fa_ref, w_ref, own_ref, a_ref, b_ref):
    first_sums(fa_ref, w_ref, own_ref)
    send_rows(own_ref, a_ref, b_ref)


def late_kernel(t_ref, fa_ref, w_ref, own_ref, all_ref):
    first = lax.axis_index("tm") == 0
    for row in range(2):
        all_ref[row, 0:2] = taps(jnp.where(first, 0.0, t_ref[row].astype(F32)))
    all_ref[:, 2:4] = fa_ref[:, 0:2]
    first_sums(all_ref, w_ref, own_ref)


def next_kernel(rb_ref, own_ref, ra_ref, bias_ref, gain_ref, w_ref, late_ref, sa_ref, q_ref, a_ref, b_ref):
    send_rows(late_ref, a_ref, b_ref)
    second_act(own_ref, rb_ref, ra_ref, bias_ref, gain_ref, sa_ref)
    both = jnp.zeros((2, 2, COLS, 192), F32)
    one = jnp.zeros((2, 1, COLS, 192), F32)
    for j in range(3):
        both += second_dot(sa_ref[j : j + 2], w_ref, 0, j)
        one += second_dot(sa_ref[j : j + 2, 1:2], w_ref, 1, j)
    q_ref[0] = jnp.concatenate([both[0, 0] + one[0, 0], both[1, 0] + one[1, 0]], axis=-1).astype(BF16)
    q_ref[1] = jnp.concatenate([both[0, 1], both[1, 1]], axis=-1).astype(BF16)


def rest_kernel(sa_ref, w_ref, x_ref, sw_ref, bias_ref, sbias_ref, acc_ref):
    bias = bias_ref[...] + sbias_ref[...]
    for row in range(2):
        skip = lax.dot_general(
            x_ref[:, row].reshape(4 * COLS, 384), sw_ref[...], (((1,), (1,)), ((), ())), preferred_element_type=F32
        )
        acc_ref[row] = skip.reshape(4, COLS, 192) + bias
    for j in range(3):
        acc_ref[:, 2:4] += second_dot(sa_ref[j : j + 2], w_ref, 2, j)
        acc_ref[:, 3:4] += second_dot(sa_ref[j : j + 2, 0:1], w_ref, 1, j)


def second_kernel(
    q_ref, rb_ref, own_ref, ra_ref, bias_ref, gain_ref, w_ref, rest_ref, out_ref, acc_ref, sa_ref
):
    second_act(own_ref, rb_ref, ra_ref, bias_ref, gain_ref, sa_ref)
    acc_ref[...] = rest_ref[...]
    for i in range(3):
        for j in range(3):
            acc_ref[:, 2 - i : 4 - i] += second_dot(sa_ref[j : j + 2], w_ref, i, j)
    came = jnp.where(lax.axis_index("tm") == 0, 0.0, q_ref[...].astype(F32))
    for row in range(2):
        out_ref[0:2, row] = (acc_ref[row, 0:2] + came[..., 192 * row : 192 * row + 192]).astype(BF16)
        out_ref[2:4, row] = acc_ref[row, 2:4].astype(BF16)


def swap_pairs(count):
    inner = [(i, i ^ 1) for i in range(count)]
    outer = [(0, 0), (count - 1, count - 1)]
    for i in range(1, count - 1, 2):
        outer += [(i, i + 1), (i + 1, i)]
    return inner, outer


def per_device(x, w1, b1, g1, w2, b2, g2, sw, sb):
    inner, outer = swap_pairs(lax.axis_size("rows"))
    steps = lax.axis_size("tm")
    ring = [(i, (i + 1) % steps) for i in range(steps)]
    w1 = jnp.swapaxes(w1, 3, 4)
    sw = jnp.swapaxes(sw, 0, 1)
    b1, b2, g2, sb = (v.reshape(1, -1) for v in (b1, b2, g2, sb))
    sums = [shape((4, 2, COLS, 192), F32), shape((2, COLS, 384)), shape((2, COLS, 384))]

    fa, give = call(
        act_kernel, [shape((2, 4, COLS, 1152)), shape((2, 2, COLS, 384))], x, g1, flops=4 * 10**9, in_hbm=(0, 1),
        scratch=[
            pltpu.VMEM((4, 2, COLS, 384), BF16), pltpu.VMEM((384,), F32),
            pltpu.SemaphoreType.DMA(()), pltpu.SemaphoreType.DMA((4,)),
        ],
    )
    came = lax.ppermute(give, "tm", ring)
    own23, edge_a, edge_b = call(early_kernel, sums, fa, w1, flops=10**9)
    b23 = lax.ppermute(edge_b, "rows", outer)
    a23 = lax.ppermute(edge_a, "rows", inner)
    own01 = call(
        late_kernel, sums[:1], came, fa, w1, flops=10**9, scratch=[pltpu.VMEM((2, 4, COLS, 1152), BF16)]
    )[0]
    sa23, give, edge_a, edge_b = call(
        next_kernel, [shape((4, 2, COLS, 576)), shape((2, COLS, 384)), *sums[1:]],
        b23, own23, a23, b1, g2, w2, own01, flops=10**9,
    )
    came = lax.ppermute(give, "tm", ring)
    b01 = lax.ppermute(edge_b, "rows", outer)
    a01 = lax.ppermute(edge_a, "rows", inner)
    rest = call(rest_kernel, [shape((2, 4, COLS, 192), F32)], sa23, w2, x, sw, b2, sb, flops=10**9)[0]
    return call(
        second_kernel, [shape((4, 2, COLS, 192))], came, b01, own01, a01, b1, g2, w2, rest, flops=10**9,
        scratch=[pltpu.VMEM((2, 4, COLS, 192), F32), pltpu.VMEM((4, 2, COLS, 576), BF16)],
    )[0]


def solution(mesh):
    return jax.shard_map(
        per_device,
        mesh=mesh,
        in_specs=(P("tm", "rows", None, None), P(), P(), P(), P(), P(), P(), P(), P()),
        out_specs=P("tm", "rows", None, None),
        check_vma=False,
    )
```

```python
import jax
import jax.numpy as jnp
from jax import lax
from jax.experimental import pallas as pl
from jax.experimental.pallas import tpu as pltpu
from jax.sharding import PartitionSpec as P

F32 = jnp.float32
BF16 = jnp.bfloat16
COLS = 64
VMEM = pl.BlockSpec(memory_space=pltpu.VMEM)
HBM = pl.BlockSpec(memory_space=pltpu.HBM)


def call(body, outs, *args, flops=0, scratch=(), limit=8, in_hbm=()):
    args = [pltpu.with_memory_space_constraint(a, pltpu.HBM) if n in in_hbm else a for n, a in enumerate(args)]
    moved = sum(a.size * a.dtype.itemsize for a in args) + sum(o.size * o.dtype.itemsize for o in outs)
    return pl.pallas_call(
        body,
        out_shape=outs,
        in_specs=[HBM if n in in_hbm else VMEM for n in range(len(args))],
        out_specs=[VMEM] * len(outs),
        scratch_shapes=list(scratch),
        compiler_params=pltpu.CompilerParams(vmem_limit_bytes=limit << 20),
        cost_estimate=pl.CostEstimate(flops=flops, bytes_accessed=moved, transcendentals=0),
    )(*args)


def shape(dims, dtype=BF16):
    return jax.ShapeDtypeStruct(dims, dtype)


def act(values, gain):
    mean = jnp.mean(values * values, axis=-1, keepdims=True)
    scaled = values * lax.rsqrt(mean + 1e-06) * gain
    return scaled / (1.0 + jnp.exp(-scaled))


def taps(values):
    frames, _, channels = values.shape
    flat = values.reshape(frames * COLS, channels)
    col = lax.broadcasted_iota(jnp.int32, flat.shape, 0) % COLS
    left = jnp.where(col == 0, 0.0, pltpu.roll(flat, 1, 0))
    right = jnp.where(col == COLS - 1, 0.0, pltpu.roll(flat, frames * COLS - 1, 0))
    return jnp.concatenate([left, flat, right], axis=-1).astype(BF16).reshape(frames, COLS, 3 * channels)


def first_sums(parts, w_ref, acc_ref):
    for i, source, frames in parts:
        count = source.shape[1]
        a = source.reshape(2 * count * COLS, 1152)
        for j in range(3):
            w = jnp.concatenate([w_ref[i, j, k] for k in range(3)], axis=-1)
            out = lax.dot_general(a, w, (((1,), (1,)), ((), ())), preferred_element_type=F32)
            acc_ref[2 - j : 4 - j, frames] += out.reshape(2, count, COLS, 192)


def edge_rows(acc_ref, outer):
    odd = lax.axis_index("rows") % 2 == 1
    up = jnp.concatenate([acc_ref[0], acc_ref[1]], axis=-1)
    down = jnp.concatenate([acc_ref[2], acc_ref[3]], axis=-1)
    return jnp.where(odd, down if outer else up, up if outer else down).astype(BF16)


def second_act(own_ref, rb_ref, ra_ref, bias_ref, gain_ref, sa_ref):
    rows = lax.axis_index("rows")
    odd = rows % 2 == 1
    a, b = ra_ref[...].astype(F32), rb_ref[...].astype(F32)
    above, below = jnp.where(odd, a, b), jnp.where(odd, b, a)
    top, bottom = rows == 0, rows == lax.axis_size("rows") - 1
    above, below = jnp.where(top, 0.0, above), jnp.where(bottom, 0.0, below)
    for row, rim in enumerate((above[..., :192], above[..., 192:], below[..., :192], below[..., 192:])):
        hidden = (own_ref[row] + rim + bias_ref[...]).astype(BF16).astype(F32)
        second = act(hidden, gain_ref[...])
        if row == 0:
            second = jnp.where(top, 0.0, second)
        if row == 3:
            second = jnp.where(bottom, 0.0, second)
        sa_ref[row] = taps(second)


def second_dot(a, w_ref, i, j):
    rows, frames = a.shape[:2]
    a = a.reshape(rows * frames * COLS, 576)
    out = jnp.dot(a, w_ref[i, j].reshape(576, 192), preferred_element_type=F32)
    return out.reshape(rows, frames, COLS, 192)


def act_kernel(x_hbm, g_hbm, fa_ref, t_ref, x_ref, g_ref, gsem, sem):
    gain_load = pltpu.make_async_copy(g_hbm, g_ref, gsem)
    loads = [pltpu.make_async_copy(x_hbm.at[t], x_ref.at[t], sem.at[t]) for t in range(4)]
    for load in [gain_load] + loads:
        load.start()
    gain_load.wait()
    gain = g_ref[...].reshape(1, 384)
    for t in range(4):
        loads[t].wait()
        for row in range(2):
            value = act(x_ref[t, row].astype(F32), gain)
            fa_ref[row, t] = taps(value[None])[0]
            if t >= 2:
                t_ref[row, t - 2] = value.astype(BF16)


def early_kernel(fa_ref, w_ref, own_ref, b_ref):
    own_ref[...] = jnp.zeros_like(own_ref)
    first_sums([(i, fa_ref[:, i : i + 2], slice(0, 2)) for i in range(3)], w_ref, own_ref)
    b_ref[...] = edge_rows(own_ref, True)


def between_kernel(own_ref, fa_ref, w_ref, part_ref, a_ref):
    a_ref[...] = edge_rows(own_ref, False)
    part_ref[...] = jnp.zeros_like(part_ref)
    parts = [(2, fa_ref[:, 0:2], slice(0, 2)), (1, fa_ref[:, 0:1], slice(1, 2))]
    first_sums(parts, w_ref, part_ref)


def late_kernel(t_ref, part_ref, w_ref, after_ref, own_ref, b_ref, fa_ref):
    del after_ref
    first = lax.axis_index("tm") == 0
    for row in range(2):
        fa_ref[row] = taps(jnp.where(first, 0.0, t_ref[row].astype(F32)))
    own_ref[...] = part_ref[...]
    parts = [(0, fa_ref[...], slice(0, 2)), (1, fa_ref[:, 1:2], slice(0, 1))]
    first_sums(parts, w_ref, own_ref)
    b_ref[...] = edge_rows(own_ref, True)


def next_kernel(rb_ref, own_ref, ra_ref, bias_ref, gain_ref, w_ref, sa_ref, q_ref):
    second_act(own_ref, rb_ref, ra_ref, bias_ref, gain_ref, sa_ref)
    both = jnp.zeros((2, 2, COLS, 192), F32)
    one = jnp.zeros((2, 1, COLS, 192), F32)
    for j in range(3):
        both += second_dot(sa_ref[j : j + 2], w_ref, 0, j)
        one += second_dot(sa_ref[j : j + 2, 1:2], w_ref, 1, j)
    q_ref[0] = jnp.concatenate([both[0, 0] + one[0, 0], both[1, 0] + one[1, 0]], axis=-1).astype(BF16)
    q_ref[1] = jnp.concatenate([both[0, 1], both[1, 1]], axis=-1).astype(BF16)


def rest_kernel(own_ref, sa_ref, w_ref, x_ref, sw_ref, bias_ref, sbias_ref, acc_ref, a_ref):
    a_ref[...] = edge_rows(own_ref, False)
    bias = bias_ref[...] + sbias_ref[...]
    for row in range(2):
        skip = lax.dot_general(
            x_ref[:, row].reshape(4 * COLS, 384), sw_ref[...], (((1,), (1,)), ((), ())), preferred_element_type=F32
        )
        acc_ref[row] = skip.reshape(4, COLS, 192) + bias
    for j in range(3):
        acc_ref[:, 2:4] += second_dot(sa_ref[j : j + 2], w_ref, 2, j)
        acc_ref[:, 3:4] += second_dot(sa_ref[j : j + 2, 0:1], w_ref, 1, j)


def second_kernel(
    q_ref, rb_ref, own_ref, ra_ref, bias_ref, gain_ref, w_ref, rest_ref, out_ref, acc_ref, sa_ref
):
    second_act(own_ref, rb_ref, ra_ref, bias_ref, gain_ref, sa_ref)
    acc_ref[...] = rest_ref[...]
    for i in range(3):
        for j in range(3):
            acc_ref[:, 2 - i : 4 - i] += second_dot(sa_ref[j : j + 2], w_ref, i, j)
    came = jnp.where(lax.axis_index("tm") == 0, 0.0, q_ref[...].astype(F32))
    for row in range(2):
        out_ref[0:2, row] = (acc_ref[row, 0:2] + came[..., 192 * row : 192 * row + 192]).astype(BF16)
        out_ref[2:4, row] = acc_ref[row, 2:4].astype(BF16)


def swap_pairs(steps, count):
    inner = [(i, i ^ 1) for i in range(count)]
    outer = []
    for t in range(steps):
        base = t * count
        for i in range(1, count - 1, 2):
            outer += [(base + i, base + i + 1), (base + i + 1, base + i)]
        for i in (0, count - 1):
            outer.append((base + i, (t ^ 1) * count + i))
    return inner, outer


def per_device(x, w1, b1, g1, w2, b2, g2, sw, sb):
    steps = lax.axis_size("tm")
    inner, outer = swap_pairs(steps, lax.axis_size("rows"))
    ring = [(i, (i + 1) % steps) for i in range(steps)]
    w1 = jnp.swapaxes(w1, 3, 4)
    sw = jnp.swapaxes(sw, 0, 1)
    b1, b2, g2, sb = (v.reshape(1, -1) for v in (b1, b2, g2, sb))
    sums, edges = shape((4, 2, COLS, 192), F32), shape((2, COLS, 384))

    fa, give = call(
        act_kernel, [shape((2, 4, COLS, 1152)), shape((2, 2, COLS, 384))], x, g1, flops=4 * 10**9, in_hbm=(0, 1),
        scratch=[
            pltpu.VMEM((4, 2, COLS, 384), BF16), pltpu.VMEM((384,), F32),
            pltpu.SemaphoreType.DMA(()), pltpu.SemaphoreType.DMA((4,)),
        ],
    )
    came = lax.ppermute(give, "tm", ring)
    own23, edge = call(early_kernel, [sums, edges], fa, w1, flops=10**9)
    b23 = lax.optimization_barrier(lax.ppermute(edge, ("tm", "rows"), outer))
    part, edge = call(between_kernel, [sums, edges], own23, fa, w1, flops=10**9)
    a23 = lax.ppermute(edge, "rows", inner)
    sa23, give = call(
        next_kernel, [shape((4, 2, COLS, 576)), edges], b23, own23, a23, b1, g2, w2, flops=10**9
    )
    q = lax.ppermute(give, "tm", ring)
    own01, edge = call(
        late_kernel, [sums, edges], came, part, w1, sa23, flops=10**9, scratch=[pltpu.VMEM((2, 2, COLS, 1152), BF16)]
    )
    b01 = lax.optimization_barrier(lax.ppermute(edge, ("tm", "rows"), outer))
    rest, edge = call(
        rest_kernel, [shape((2, 4, COLS, 192), F32), edges], own01, sa23, w2, x, sw, b2, sb, flops=10**9
    )
    a01 = lax.ppermute(edge, "rows", inner)
    return call(
        second_kernel, [shape((4, 2, COLS, 192))], q, b01, own01, a01, b1, g2, w2, rest, flops=10**9,
        scratch=[pltpu.VMEM((2, 4, COLS, 192), F32), pltpu.VMEM((4, 2, COLS, 576), BF16)],
    )[0]


def solution(mesh):
    return jax.shard_map(
        per_device,
        mesh=mesh,
        in_specs=(P("tm", "rows", None, None), P(), P(), P(), P(), P(), P(), P(), P()),
        out_specs=P("tm", "rows", None, None),
        check_vma=False,
    )
```

```python
import jax
import jax.numpy as jnp
from jax import lax
from jax.experimental import pallas as pl
from jax.experimental.pallas import tpu as pltpu
from jax.sharding import PartitionSpec as P

F32 = jnp.float32
BF16 = jnp.bfloat16
COLS = 64
VMEM = pl.BlockSpec(memory_space=pltpu.VMEM)
HBM = pl.BlockSpec(memory_space=pltpu.HBM)


def call(body, outs, *args, flops=0, scratch=(), limit=8, in_hbm=()):
    args = [pltpu.with_memory_space_constraint(a, pltpu.HBM) if n in in_hbm else a for n, a in enumerate(args)]
    moved = sum(a.size * a.dtype.itemsize for a in args) + sum(o.size * o.dtype.itemsize for o in outs)
    return pl.pallas_call(
        body,
        out_shape=outs,
        in_specs=[HBM if n in in_hbm else VMEM for n in range(len(args))],
        out_specs=[VMEM] * len(outs),
        scratch_shapes=list(scratch),
        compiler_params=pltpu.CompilerParams(vmem_limit_bytes=limit << 20),
        cost_estimate=pl.CostEstimate(flops=flops // 10, bytes_accessed=moved // 10, transcendentals=0),
    )(*args)


def shape(dims, dtype=BF16):
    return jax.ShapeDtypeStruct(dims, dtype)


def act(values, gain):
    mean = jnp.mean(values * values, axis=-1, keepdims=True)
    scaled = values * lax.rsqrt(mean + 1e-06) * gain
    return scaled / (1.0 + jnp.exp(-scaled))


def taps(values):
    frames, _, channels = values.shape
    flat = values.reshape(frames * COLS, channels)
    col = lax.broadcasted_iota(jnp.int32, flat.shape, 0) % COLS
    left = jnp.where(col == 0, 0.0, pltpu.roll(flat, 1, 0))
    right = jnp.where(col == COLS - 1, 0.0, pltpu.roll(flat, frames * COLS - 1, 0))
    return jnp.concatenate([left, flat, right], axis=-1).astype(BF16).reshape(frames, COLS, 3 * channels)


def first_sums(parts, w_ref, acc_ref):
    for i, source, frames in parts:
        count = source.shape[1]
        a = source.reshape(2 * count * COLS, 1152)
        for j in range(3):
            w = jnp.concatenate([w_ref[i, j, k] for k in range(3)], axis=-1)
            out = lax.dot_general(a, w, (((1,), (1,)), ((), ())), preferred_element_type=F32)
            acc_ref[2 - j : 4 - j, frames] += out.reshape(2, count, COLS, 192)


def edge_rows(acc_ref, outer):
    odd = lax.axis_index("rows") % 2 == 1
    up = jnp.concatenate([acc_ref[0], acc_ref[1]], axis=-1)
    down = jnp.concatenate([acc_ref[2], acc_ref[3]], axis=-1)
    return jnp.where(odd, down if outer else up, up if outer else down).astype(BF16)


def outer_side():
    return lax.axis_index("rows") % 2


def second_act(own_ref, r_ref, bias_ref, gain_ref, side, outer, sa_ref):
    rows = lax.axis_index("rows")
    edge = jnp.logical_or(rows == 0, rows == lax.axis_size("rows") - 1)
    came = r_ref[...].astype(F32)
    if outer:
        came = jnp.where(edge, 0.0, came)
    for n in range(2):
        hidden = own_ref[2 * side + n] + came[..., 192 * n : 192 * n + 192] + bias_ref[...]
        second = act(hidden.astype(BF16).astype(F32), gain_ref[...])
        if outer:
            second = jnp.where(jnp.logical_and(edge, side == n), 0.0, second)
        sa_ref[n] = taps(second)


def second_sums(sa_ref, w_ref, side, parts, acc_ref):
    def dot(a, w):
        count = a.shape[0] * a.shape[1]
        out = jnp.dot(a.reshape(count * COLS, 576), w.reshape(576, 192), preferred_element_type=F32)
        return out.reshape(a.shape[0], a.shape[1], COLS, 192)

    for i, source, frames in parts:
        acc_ref[:, frames] += dot(sa_ref[:, source], w_ref[i, 2 * side])
        acc_ref[pl.ds(side, 1), frames] += dot(sa_ref[pl.ds(1 - side, 1), source], w_ref[i, 1])


def act_kernel(x_hbm, g_hbm, fa_ref, t_ref, x_ref, g_ref, gsem, sem):
    gain_load = pltpu.make_async_copy(g_hbm, g_ref, gsem)
    loads = [pltpu.make_async_copy(x_hbm.at[t], x_ref.at[t], sem.at[t]) for t in range(4)]
    for load in [gain_load] + loads:
        load.start()
    gain_load.wait()
    gain = g_ref[...].reshape(1, 384)
    for t in range(4):
        loads[t].wait()
        for row in range(2):
            value = act(x_ref[t, row].astype(F32), gain)
            fa_ref[row, t] = taps(value[None])[0]
            if t >= 2:
                t_ref[row, t - 2] = value.astype(BF16)


def early_kernel(fa_ref, w_ref, own_ref, a_ref, b_ref):
    own_ref[...] = jnp.zeros_like(own_ref)
    first_sums([(i, fa_ref[:, i : i + 2], slice(0, 2)) for i in range(3)], w_ref, own_ref)
    a_ref[...] = edge_rows(own_ref, False)
    b_ref[...] = edge_rows(own_ref, True)


def between_kernel(fa_ref, w_ref, part_ref):
    part_ref[...] = jnp.zeros_like(part_ref)
    parts = [(2, fa_ref[:, 0:2], slice(0, 2)), (1, fa_ref[:, 0:1], slice(1, 2))]
    first_sums(parts, w_ref, part_ref)


def late_kernel(t_ref, part_ref, w_ref, after_ref, own_ref, a_ref, b_ref, fa_ref):
    del after_ref
    first = lax.axis_index("tm") == 0
    for row in range(2):
        fa_ref[row] = taps(jnp.where(first, 0.0, t_ref[row].astype(F32)))
    own_ref[...] = part_ref[...]
    parts = [(0, fa_ref[...], slice(0, 2)), (1, fa_ref[:, 1:2], slice(0, 1))]
    first_sums(parts, w_ref, own_ref)
    a_ref[...] = edge_rows(own_ref, False)
    b_ref[...] = edge_rows(own_ref, True)


NEXT = [(0, slice(0, 2), slice(0, 2)), (1, slice(1, 2), slice(0, 1))]
REST = [(2, slice(0, 2), slice(2, 4)), (1, slice(0, 1), slice(3, 4))]
FIRST = [(i, slice(0, 2), slice(2 - i, 4 - i)) for i in range(3)]


def near_kernel(ra_ref, own_ref, bias_ref, gain_ref, w_ref, sa_ref, q_ref):
    side = 1 - outer_side()
    second_act(own_ref, ra_ref, bias_ref, gain_ref, side, False, sa_ref)
    q_ref[...] = jnp.zeros_like(q_ref)
    second_sums(sa_ref, w_ref, side, NEXT, q_ref)


def next_kernel(rb_ref, own_ref, part_ref, bias_ref, gain_ref, w_ref, sa_ref, q_ref, acc_ref):
    side = outer_side()
    second_act(own_ref, rb_ref, bias_ref, gain_ref, side, True, sa_ref)
    acc_ref[...] = part_ref[...]
    second_sums(sa_ref, w_ref, side, NEXT, acc_ref)
    q_ref[...] = jnp.concatenate([acc_ref[0], acc_ref[1]], axis=-1).astype(BF16)


def rest_kernel(near_ref, far_ref, w_ref, x_ref, sw_ref, bias_ref, sbias_ref, acc_ref):
    bias = bias_ref[...] + sbias_ref[...]
    for row in range(2):
        skip = lax.dot_general(
            x_ref[:, row].reshape(4 * COLS, 384), sw_ref[...], (((1,), (1,)), ((), ())), preferred_element_type=F32
        )
        acc_ref[row] = skip.reshape(4, COLS, 192) + bias
    second_sums(near_ref, w_ref, 1 - outer_side(), REST, acc_ref)
    second_sums(far_ref, w_ref, outer_side(), REST, acc_ref)


def second_near_kernel(ra_ref, own_ref, bias_ref, gain_ref, w_ref, rest_ref, acc_ref, sa_ref):
    side = 1 - outer_side()
    second_act(own_ref, ra_ref, bias_ref, gain_ref, side, False, sa_ref)
    acc_ref[...] = rest_ref[...]
    second_sums(sa_ref, w_ref, side, FIRST, acc_ref)


def second_kernel(q_ref, rb_ref, own_ref, part_ref, bias_ref, gain_ref, w_ref, out_ref, acc_ref, sa_ref):
    side = outer_side()
    second_act(own_ref, rb_ref, bias_ref, gain_ref, side, True, sa_ref)
    acc_ref[...] = part_ref[...]
    second_sums(sa_ref, w_ref, side, FIRST, acc_ref)
    came = jnp.where(lax.axis_index("tm") == 0, 0.0, q_ref[...].astype(F32))
    for row in range(2):
        out_ref[0:2, row] = (acc_ref[row, 0:2] + came[..., 192 * row : 192 * row + 192]).astype(BF16)
        out_ref[2:4, row] = acc_ref[row, 2:4].astype(BF16)


def swap_pairs(steps, count):
    inner = [(i, i ^ 1) for i in range(count)]
    outer = []
    for t in range(steps):
        base = t * count
        for i in range(1, count - 1, 2):
            outer += [(base + i, base + i + 1), (base + i + 1, base + i)]
        for i in (0, count - 1):
            outer.append((base + i, (t ^ 1) * count + i))
    return inner, outer


def per_device(x, w1, b1, g1, w2, b2, g2, sw, sb):
    steps = lax.axis_size("tm")
    inner, outer = swap_pairs(steps, lax.axis_size("rows"))
    ring = [(i, (i + 1) % steps) for i in range(steps)]
    w1 = jnp.swapaxes(w1, 3, 4)
    sw = jnp.swapaxes(sw, 0, 1)
    b1, b2, g2, sb = (v.reshape(1, -1) for v in (b1, b2, g2, sb))
    half = shape((2, 2, COLS, 576))
    sums, edges = shape((4, 2, COLS, 192), F32), shape((2, COLS, 384))

    fa, give = call(
        act_kernel, [shape((2, 4, COLS, 1152)), shape((2, 2, COLS, 384))], x, g1, flops=4 * 10**10, in_hbm=(0, 1),
        scratch=[
            pltpu.VMEM((4, 2, COLS, 384), BF16), pltpu.VMEM((384,), F32),
            pltpu.SemaphoreType.DMA(()), pltpu.SemaphoreType.DMA((4,)),
        ],
    )
    came = lax.ppermute(give, "tm", ring)
    own23, edge_a, edge_b = call(early_kernel, [sums, edges, edges], fa, w1, flops=10**9)
    b23 = lax.ppermute(edge_b, ("tm", "rows"), outer)
    a23 = lax.ppermute(edge_a, "rows", inner)
    part = call(between_kernel, [sums], fa, w1, flops=10**9)[0]
    near, part_q = call(near_kernel, [half, shape((2, 2, COLS, 192), F32)], a23, own23, b1, g2, w2, flops=10**9)
    far, give = call(
        next_kernel, [half, edges], b23, own23, part_q, b1, g2, w2, flops=10**9,
        scratch=[pltpu.VMEM((2, 2, COLS, 192), F32)],
    )
    q = lax.optimization_barrier(lax.ppermute(give, "tm", ring))
    own01, edge_a, edge_b = call(
        late_kernel, [sums, edges, edges], came, part, w1, far, flops=10**9,
        scratch=[pltpu.VMEM((2, 2, COLS, 1152), BF16)],
    )
    b01 = lax.ppermute(edge_b, ("tm", "rows"), outer)
    a01 = lax.ppermute(edge_a, "rows", inner)
    rest = call(rest_kernel, [shape((2, 4, COLS, 192), F32)], near, far, w2, x, sw, b2, sb, flops=10**9)[0]
    total = call(
        second_near_kernel, [shape((2, 4, COLS, 192), F32)], a01, own01, b1, g2, w2, rest, flops=10**9,
        scratch=[pltpu.VMEM((2, 2, COLS, 576), BF16)],
    )[0]
    return call(
        second_kernel, [shape((4, 2, COLS, 192))], q, b01, own01, total, b1, g2, w2, flops=10**9,
        scratch=[pltpu.VMEM((2, 4, COLS, 192), F32), pltpu.VMEM((2, 2, COLS, 576), BF16)],
    )[0]


def solution(mesh):
    return jax.shard_map(
        per_device,
        mesh=mesh,
        in_specs=(P("tm", "rows", None, None), P(), P(), P(), P(), P(), P(), P(), P()),
        out_specs=P("tm", "rows", None, None),
        check_vma=False,
    )
```

```python
import jax
import jax.numpy as jnp
from jax import lax
from jax.experimental import pallas as pl
from jax.experimental.pallas import tpu as pltpu
from jax.sharding import PartitionSpec as P

F32 = jnp.float32
BF16 = jnp.bfloat16
COLS = 64
VMEM = pl.BlockSpec(memory_space=pltpu.VMEM)
HBM = pl.BlockSpec(memory_space=pltpu.HBM)


def call(body, outs, *args, flops=0, scratch=(), limit=8, in_hbm=()):
    args = [pltpu.with_memory_space_constraint(a, pltpu.HBM) if n in in_hbm else a for n, a in enumerate(args)]
    moved = sum(a.size * a.dtype.itemsize for a in args) + sum(o.size * o.dtype.itemsize for o in outs)
    return pl.pallas_call(
        body,
        out_shape=outs,
        in_specs=[HBM if n in in_hbm else VMEM for n in range(len(args))],
        out_specs=[VMEM] * len(outs),
        scratch_shapes=list(scratch),
        compiler_params=pltpu.CompilerParams(vmem_limit_bytes=limit << 20),
        cost_estimate=pl.CostEstimate(flops=flops // 10, bytes_accessed=moved // 10, transcendentals=0),
    )(*args)


def shape(dims, dtype=BF16):
    return jax.ShapeDtypeStruct(dims, dtype)


def act(values, gain):
    mean = jnp.mean(values * values, axis=-1, keepdims=True)
    scaled = values * lax.rsqrt(mean + 1e-06) * gain
    half = 0.5 * scaled
    return half + half * jnp.tanh(half)


def taps(values):
    frames, _, channels = values.shape
    flat = values.reshape(frames * COLS, channels)
    col = lax.broadcasted_iota(jnp.int32, flat.shape, 0) % COLS
    left = jnp.where(col == 0, 0.0, pltpu.roll(flat, 1, 0))
    right = jnp.where(col == COLS - 1, 0.0, pltpu.roll(flat, frames * COLS - 1, 0))
    return jnp.concatenate([left, flat, right], axis=-1).astype(BF16).reshape(frames, COLS, 3 * channels)


def first_sums(parts, w_ref):
    a = jnp.concatenate([source.reshape(4 * COLS, 1152) for _, source in parts], axis=-1)
    outs = []
    for j in range(3):
        w = jnp.concatenate([w_ref[i, j, k] for i, _ in parts for k in range(3)], axis=-1)
        out = lax.dot_general(a, w, (((1,), (1,)), ((), ())), preferred_element_type=F32)
        outs.append(out.reshape(2, 2, COLS, 192))
    return outs[2][0], outs[2][1] + outs[1][0], outs[1][1] + outs[0][0], outs[0][1]


def edge_rows(acc_ref, outer):
    odd = lax.axis_index("rows") % 2 == 1
    up = jnp.concatenate([acc_ref[0], acc_ref[1]], axis=-1)
    down = jnp.concatenate([acc_ref[2], acc_ref[3]], axis=-1)
    return jnp.where(odd, down if outer else up, up if outer else down).astype(BF16)


def outer_side():
    return lax.axis_index("rows") % 2


def second_act(own_ref, r_ref, bias_ref, gain_ref, side, outer, sa_ref):
    rows = lax.axis_index("rows")
    edge = jnp.logical_or(rows == 0, rows == lax.axis_size("rows") - 1)
    came = r_ref[...].astype(F32)
    if outer:
        came = jnp.where(edge, 0.0, came)
    for n in range(2):
        hidden = own_ref[2 * side + n] + came[..., 192 * n : 192 * n + 192] + bias_ref[...]
        second = act(hidden.astype(BF16).astype(F32), gain_ref[...])
        if outer:
            second = jnp.where(jnp.logical_and(edge, side == n), 0.0, second)
        sa_ref[n] = taps(second)


def second_sums(sa_ref, w_ref, side, parts, acc_ref):
    def dot(a, w):
        count = a.shape[0] * a.shape[1]
        out = jnp.dot(a.reshape(count * COLS, 576), w.reshape(576, 192), preferred_element_type=F32)
        return out.reshape(a.shape[0], a.shape[1], COLS, 192)

    for i, source, frames in parts:
        acc_ref[:, frames] += dot(sa_ref[:, source], w_ref[i, 2 * side])
        acc_ref[pl.ds(side, 1), frames] += dot(sa_ref[pl.ds(1 - side, 1), source], w_ref[i, 1])


def act_kernel(x_hbm, g_hbm, fa_ref, t_ref, x_ref, g_ref, gsem, sem):
    gain_load = pltpu.make_async_copy(g_hbm, g_ref, gsem)
    loads = [pltpu.make_async_copy(x_hbm.at[t], x_ref.at[t], sem.at[t]) for t in range(4)]
    for load in [gain_load] + loads:
        load.start()
    gain_load.wait()
    gain = g_ref[...].reshape(1, 384)
    for t in range(4):
        loads[t].wait()
        for row in range(2):
            value = act(x_ref[t, row].astype(F32), gain)
            fa_ref[row, t] = taps(value[None])[0]
            if t >= 2:
                t_ref[row, t - 2] = value.astype(BF16)


def early_kernel(fa_ref, w_ref, own_ref, a_ref, b_ref):
    for row, total in enumerate(first_sums([(i, fa_ref[:, i : i + 2]) for i in range(3)], w_ref)):
        own_ref[row] = total
    a_ref[...] = edge_rows(own_ref, False)
    b_ref[...] = edge_rows(own_ref, True)


def between_kernel(fa_ref, w_ref, part_ref):
    first = fa_ref[:, 0:1]
    parts = [(2, fa_ref[:, 0:2]), (1, jnp.concatenate([jnp.zeros_like(first), first], axis=1))]
    for row, total in enumerate(first_sums(parts, w_ref)):
        part_ref[row] = total


def late_kernel(t_ref, part_ref, w_ref, after_ref, own_ref, a_ref, b_ref, fa_ref):
    del after_ref
    first = lax.axis_index("tm") == 0
    for row in range(2):
        fa_ref[row] = taps(jnp.where(first, 0.0, t_ref[row].astype(F32)))
    last = fa_ref[:, 1:2]
    parts = [(0, fa_ref[...]), (1, jnp.concatenate([last, jnp.zeros_like(last)], axis=1))]
    for row, total in enumerate(first_sums(parts, w_ref)):
        own_ref[row] = part_ref[row] + total
    a_ref[...] = edge_rows(own_ref, False)
    b_ref[...] = edge_rows(own_ref, True)


NEXT = [(0, slice(0, 2), slice(0, 2)), (1, slice(1, 2), slice(0, 1))]
REST = [(2, slice(0, 2), slice(2, 4)), (1, slice(0, 1), slice(3, 4))]
FIRST = [(i, slice(0, 2), slice(2 - i, 4 - i)) for i in range(3)]


def near_kernel(ra_ref, own_ref, bias_ref, gain_ref, w_ref, sa_ref, q_ref):
    side = 1 - outer_side()
    second_act(own_ref, ra_ref, bias_ref, gain_ref, side, False, sa_ref)
    q_ref[...] = jnp.zeros_like(q_ref)
    second_sums(sa_ref, w_ref, side, NEXT, q_ref)


def next_kernel(rb_ref, own_ref, part_ref, bias_ref, gain_ref, w_ref, sa_ref, q_ref, acc_ref):
    side = outer_side()
    second_act(own_ref, rb_ref, bias_ref, gain_ref, side, True, sa_ref)
    acc_ref[...] = part_ref[...]
    second_sums(sa_ref, w_ref, side, NEXT, acc_ref)
    q_ref[...] = jnp.concatenate([acc_ref[0], acc_ref[1]], axis=-1).astype(BF16)


def rest_kernel(near_ref, far_ref, w_ref, x_ref, sw_ref, bias_ref, sbias_ref, acc_ref):
    bias = bias_ref[...] + sbias_ref[...]
    for row in range(2):
        skip = lax.dot_general(
            x_ref[:, row].reshape(4 * COLS, 384), sw_ref[...], (((1,), (1,)), ((), ())), preferred_element_type=F32
        )
        acc_ref[row] = skip.reshape(4, COLS, 192) + bias
    second_sums(near_ref, w_ref, 1 - outer_side(), REST, acc_ref)
    second_sums(far_ref, w_ref, outer_side(), REST, acc_ref)


def second_near_kernel(ra_ref, own_ref, bias_ref, gain_ref, w_ref, rest_ref, acc_ref, sa_ref):
    side = 1 - outer_side()
    second_act(own_ref, ra_ref, bias_ref, gain_ref, side, False, sa_ref)
    acc_ref[...] = rest_ref[...]
    second_sums(sa_ref, w_ref, side, FIRST, acc_ref)


def second_kernel(q_ref, rb_ref, own_ref, part_ref, bias_ref, gain_ref, w_ref, out_ref, acc_ref, sa_ref):
    side = outer_side()
    second_act(own_ref, rb_ref, bias_ref, gain_ref, side, True, sa_ref)
    acc_ref[...] = part_ref[...]
    second_sums(sa_ref, w_ref, side, FIRST, acc_ref)
    came = jnp.where(lax.axis_index("tm") == 0, 0.0, q_ref[...].astype(F32))
    for row in range(2):
        out_ref[0:2, row] = (acc_ref[row, 0:2] + came[..., 192 * row : 192 * row + 192]).astype(BF16)
        out_ref[2:4, row] = acc_ref[row, 2:4].astype(BF16)


def swap_pairs(steps, count):
    inner = [(i, i ^ 1) for i in range(count)]
    outer = []
    for t in range(steps):
        base = t * count
        for i in range(1, count - 1, 2):
            outer += [(base + i, base + i + 1), (base + i + 1, base + i)]
        for i in (0, count - 1):
            outer.append((base + i, (t ^ 1) * count + i))
    return inner, outer


def per_device(x, w1, b1, g1, w2, b2, g2, sw, sb):
    steps = lax.axis_size("tm")
    inner, outer = swap_pairs(steps, lax.axis_size("rows"))
    ring = [(i, (i + 1) % steps) for i in range(steps)]
    w1 = jnp.swapaxes(w1, 3, 4)
    sw = jnp.swapaxes(sw, 0, 1)
    b1, b2, g2, sb = (v.reshape(1, -1) for v in (b1, b2, g2, sb))
    half = shape((2, 2, COLS, 576))
    sums, edges = shape((4, 2, COLS, 192), F32), shape((2, COLS, 384))

    fa, give = call(
        act_kernel, [shape((2, 4, COLS, 1152)), shape((2, 2, COLS, 384))], x, g1, flops=4 * 10**10, in_hbm=(0, 1),
        scratch=[
            pltpu.VMEM((4, 2, COLS, 384), BF16), pltpu.VMEM((384,), F32),
            pltpu.SemaphoreType.DMA(()), pltpu.SemaphoreType.DMA((4,)),
        ],
    )
    came = lax.ppermute(give, "tm", ring)
    own23, edge_a, edge_b = call(early_kernel, [sums, edges, edges], fa, w1, flops=10**9)
    b23 = lax.ppermute(edge_b, ("tm", "rows"), outer)
    a23 = lax.ppermute(edge_a, "rows", inner)
    part = call(between_kernel, [sums], fa, w1, flops=16*10**9)[0]
    near, part_q = call(near_kernel, [half, shape((2, 2, COLS, 192), F32)], a23, own23, b1, g2, w2, flops=10**9)
    far, give = call(
        next_kernel, [half, edges], b23, own23, part_q, b1, g2, w2, flops=10**9,
        scratch=[pltpu.VMEM((2, 2, COLS, 192), F32)],
    )
    q = lax.ppermute(give, "tm", ring)
    own01, edge_a, edge_b = call(
        late_kernel, [sums, edges, edges], came, part, w1, far, flops=10**9,
        scratch=[pltpu.VMEM((2, 2, COLS, 1152), BF16)],
    )
    b01 = lax.ppermute(edge_b, ("tm", "rows"), outer)
    a01 = lax.ppermute(edge_a, "rows", inner)
    rest = call(rest_kernel, [shape((2, 4, COLS, 192), F32)], near, far, w2, x, sw, b2, sb, flops=16*10**9)[0]
    total = call(
        second_near_kernel, [shape((2, 4, COLS, 192), F32)], a01, own01, b1, g2, w2, rest, flops=10**9,
        scratch=[pltpu.VMEM((2, 2, COLS, 576), BF16)],
    )[0]
    return call(
        second_kernel, [shape((4, 2, COLS, 192))], q, b01, own01, total, b1, g2, w2, flops=10**9,
        scratch=[pltpu.VMEM((2, 4, COLS, 192), F32), pltpu.VMEM((2, 2, COLS, 576), BF16)],
    )[0]


def solution(mesh):
    return jax.shard_map(
        per_device,
        mesh=mesh,
        in_specs=(P("tm", "rows", None, None), P(), P(), P(), P(), P(), P(), P(), P()),
        out_specs=P("tm", "rows", None, None),
        check_vma=False,
    )
```

```python
import jax
import jax.numpy as jnp
from jax import lax
from jax.experimental import pallas as pl
from jax.experimental.pallas import tpu as pltpu
from jax.sharding import PartitionSpec as P

F32 = jnp.float32
BF16 = jnp.bfloat16
COLS = 64
VMEM = pl.BlockSpec(memory_space=pltpu.VMEM)
HBM = pl.BlockSpec(memory_space=pltpu.HBM)


def call(body, outs, *args, flops=0, scratch=(), limit=8, in_hbm=()):
    args = [pltpu.with_memory_space_constraint(a, pltpu.HBM) if n in in_hbm else a for n, a in enumerate(args)]
    moved = sum(a.size * a.dtype.itemsize for a in args) + sum(o.size * o.dtype.itemsize for o in outs)
    return pl.pallas_call(
        body,
        out_shape=outs,
        in_specs=[HBM if n in in_hbm else VMEM for n in range(len(args))],
        out_specs=[VMEM] * len(outs),
        scratch_shapes=list(scratch),
        compiler_params=pltpu.CompilerParams(vmem_limit_bytes=limit << 20),
        cost_estimate=pl.CostEstimate(flops=flops // 10, bytes_accessed=moved // 10, transcendentals=0),
    )(*args)


def shape(dims, dtype=BF16):
    return jax.ShapeDtypeStruct(dims, dtype)


def act(values, gain):
    mean = jnp.mean(values * values, axis=-1, keepdims=True)
    scaled = values * lax.rsqrt(mean + 1e-06) * gain
    half = 0.5 * scaled
    return half + half * jnp.tanh(half)


def taps(values):
    frames, _, channels = values.shape
    flat = values.reshape(frames * COLS, channels)
    col = lax.broadcasted_iota(jnp.int32, flat.shape, 0) % COLS
    left = jnp.where(col == 0, 0.0, pltpu.roll(flat, 1, 0))
    right = jnp.where(col == COLS - 1, 0.0, pltpu.roll(flat, frames * COLS - 1, 0))
    return jnp.concatenate([left, flat, right], axis=-1).astype(BF16).reshape(frames, COLS, 3 * channels)


def first_dot(parts, w_ref, j):
    a = jnp.concatenate([source.reshape(4 * COLS, 1152) for _, source in parts], axis=-1)
    w = jnp.concatenate([w_ref[i, j, k] for i, _ in parts for k in range(3)], axis=-1)
    out = lax.dot_general(a, w, (((1,), (1,)), ((), ())), preferred_element_type=F32)
    return out.reshape(2, 2, COLS, 192)


def edge_rows(acc_ref):
    return jnp.concatenate([acc_ref[0], acc_ref[1]], axis=-1).astype(BF16)


def outer_side():
    return lax.axis_index("rows") % 2


def second_act(own_ref, r_ref, bias_ref, gain_ref, side, outer, sa_ref):
    rows = lax.axis_index("rows")
    edge = jnp.logical_or(rows == 0, rows == lax.axis_size("rows") - 1)
    came = r_ref[...].astype(F32)
    if outer:
        came = jnp.where(edge, 0.0, came)
    for n in range(2):
        hidden = own_ref[n] + came[..., 192 * n : 192 * n + 192] + bias_ref[...]
        second = act(hidden.astype(BF16).astype(F32), gain_ref[...])
        if outer:
            second = jnp.where(jnp.logical_and(edge, side == n), 0.0, second)
        sa_ref[n] = taps(second)


def second_sums(sa_ref, w_ref, side, parts, acc_ref):
    def dot(a, w):
        count = a.shape[0] * a.shape[1]
        out = jnp.dot(a.reshape(count * COLS, 576), w.reshape(576, 192), preferred_element_type=F32)
        return out.reshape(a.shape[0], a.shape[1], COLS, 192)

    for i, source, frames in parts:
        acc_ref[:, frames] += dot(sa_ref[:, source], w_ref[i, 2 * side])
        acc_ref[pl.ds(side, 1), frames] += dot(sa_ref[pl.ds(1 - side, 1), source], w_ref[i, 1])


def act_kernel(x_hbm, g_hbm, fa_ref, t_ref, x_ref, g_ref, gsem, sem):
    gain_load = pltpu.make_async_copy(g_hbm, g_ref, gsem)
    loads = [pltpu.make_async_copy(x_hbm.at[t], x_ref.at[t], sem.at[t]) for t in range(4)]
    for load in [gain_load] + loads:
        load.start()
    gain_load.wait()
    gain = g_ref[...].reshape(1, 384)
    for t in range(4):
        loads[t].wait()
        for row in range(2):
            value = act(x_ref[t, row].astype(F32), gain)
            fa_ref[row, t] = taps(value[None])[0]
            if t >= 2:
                t_ref[row, t - 2] = value.astype(BF16)


def early_kernel(fa_ref, w_ref, far_ref, near_ref, a_ref, b_ref, mid_ref):
    side = outer_side()
    parts = [(i, fa_ref[:, i : i + 2]) for i in range(3)]
    far_ref[...] = first_dot(parts, w_ref, 2 - 2 * side)
    mid_ref[...] = first_dot(parts, w_ref, 1)
    near_ref[...] = first_dot(parts, w_ref, 2 * side)
    far_ref[pl.ds(1 - side, 1)] += mid_ref[pl.ds(side, 1)]
    near_ref[pl.ds(side, 1)] += mid_ref[pl.ds(1 - side, 1)]
    a_ref[...] = edge_rows(near_ref)
    b_ref[...] = edge_rows(far_ref)


def between_kernel(fa_ref, w_ref, part_ref):
    side = outer_side()
    first = fa_ref[:, 0:1]
    parts = [(2, fa_ref[:, 0:2]), (1, jnp.concatenate([jnp.zeros_like(first), first], axis=1))]
    for n, j in enumerate((2 - 2 * side, 1, 2 * side)):
        part_ref[n] = first_dot(parts, w_ref, j)


def before(fa_ref):
    last = fa_ref[:, 1:2]
    return [(0, fa_ref[...]), (1, jnp.concatenate([last, jnp.zeros_like(last)], axis=1))]


def late_kernel(t_ref, part_ref, w_ref, after_ref, fa_ref, far_ref, mid_ref, b_ref):
    del after_ref
    first = lax.axis_index("tm") == 0
    side = outer_side()
    for row in range(2):
        fa_ref[row] = taps(jnp.where(first, 0.0, t_ref[row].astype(F32)))
    far_ref[...] = part_ref[0] + first_dot(before(fa_ref), w_ref, 2 - 2 * side)
    mid_ref[...] = part_ref[1] + first_dot(before(fa_ref), w_ref, 1)
    far_ref[pl.ds(1 - side, 1)] += mid_ref[pl.ds(side, 1)]
    b_ref[...] = edge_rows(far_ref)


def inner_kernel(fa_ref, mid_ref, part_ref, w_ref, near_ref, a_ref):
    side = outer_side()
    near_ref[...] = part_ref[2] + first_dot(before(fa_ref), w_ref, 2 * side)
    near_ref[pl.ds(side, 1)] += mid_ref[pl.ds(1 - side, 1)]
    a_ref[...] = edge_rows(near_ref)


NEXT = [(0, slice(0, 2), slice(0, 2)), (1, slice(1, 2), slice(0, 1))]
REST = [(2, slice(0, 2), slice(2, 4)), (1, slice(0, 1), slice(3, 4))]
FIRST = [(i, slice(0, 2), slice(2 - i, 4 - i)) for i in range(3)]


def near_kernel(ra_ref, own_ref, bias_ref, gain_ref, w_ref, sa_ref, q_ref):
    side = 1 - outer_side()
    second_act(own_ref, ra_ref, bias_ref, gain_ref, side, False, sa_ref)
    q_ref[...] = jnp.zeros_like(q_ref)
    second_sums(sa_ref, w_ref, side, NEXT, q_ref)


def next_kernel(rb_ref, own_ref, part_ref, bias_ref, gain_ref, w_ref, sa_ref, q_ref, acc_ref):
    side = outer_side()
    second_act(own_ref, rb_ref, bias_ref, gain_ref, side, True, sa_ref)
    acc_ref[...] = part_ref[...]
    second_sums(sa_ref, w_ref, side, NEXT, acc_ref)
    q_ref[...] = jnp.concatenate([acc_ref[0], acc_ref[1]], axis=-1).astype(BF16)


def rest_kernel(near_ref, far_ref, w_ref, x_ref, sw_ref, bias_ref, sbias_ref, acc_ref):
    bias = bias_ref[...] + sbias_ref[...]
    for row in range(2):
        skip = lax.dot_general(
            x_ref[:, row].reshape(4 * COLS, 384), sw_ref[...], (((1,), (1,)), ((), ())), preferred_element_type=F32
        )
        acc_ref[row] = skip.reshape(4, COLS, 192) + bias
    second_sums(near_ref, w_ref, 1 - outer_side(), REST, acc_ref)
    second_sums(far_ref, w_ref, outer_side(), REST, acc_ref)


def second_near_kernel(ra_ref, own_ref, bias_ref, gain_ref, w_ref, rest_ref, acc_ref, sa_ref):
    side = 1 - outer_side()
    second_act(own_ref, ra_ref, bias_ref, gain_ref, side, False, sa_ref)
    acc_ref[...] = rest_ref[...]
    second_sums(sa_ref, w_ref, side, FIRST, acc_ref)


def second_kernel(q_ref, rb_ref, own_ref, part_ref, bias_ref, gain_ref, w_ref, out_ref, acc_ref, sa_ref):
    side = outer_side()
    second_act(own_ref, rb_ref, bias_ref, gain_ref, side, True, sa_ref)
    acc_ref[...] = part_ref[...]
    second_sums(sa_ref, w_ref, side, FIRST, acc_ref)
    came = jnp.where(lax.axis_index("tm") == 0, 0.0, q_ref[...].astype(F32))
    for row in range(2):
        out_ref[0:2, row] = (acc_ref[row, 0:2] + came[..., 192 * row : 192 * row + 192]).astype(BF16)
        out_ref[2:4, row] = acc_ref[row, 2:4].astype(BF16)


def swap_pairs(steps, count):
    inner = [(i, i ^ 1) for i in range(count)]
    outer = []
    for t in range(steps):
        base = t * count
        for i in range(1, count - 1, 2):
            outer += [(base + i, base + i + 1), (base + i + 1, base + i)]
        for i in (0, count - 1):
            outer.append((base + i, (t ^ 1) * count + i))
    return inner, outer


def per_device(x, w1, b1, g1, w2, b2, g2, sw, sb):
    steps = lax.axis_size("tm")
    inner, outer = swap_pairs(steps, lax.axis_size("rows"))
    ring = [(i, (i + 1) % steps) for i in range(steps)]
    w1 = jnp.swapaxes(w1, 3, 4)
    sw = jnp.swapaxes(sw, 0, 1)
    b1, b2, g2, sb = (v.reshape(1, -1) for v in (b1, b2, g2, sb))
    half = shape((2, 2, COLS, 576))
    sums, edges = shape((2, 2, COLS, 192), F32), shape((2, COLS, 384))

    fa, give = call(
        act_kernel, [shape((2, 4, COLS, 1152)), shape((2, 2, COLS, 384))], x, g1, flops=4 * 10**10, in_hbm=(0, 1),
        scratch=[
            pltpu.VMEM((4, 2, COLS, 384), BF16), pltpu.VMEM((384,), F32),
            pltpu.SemaphoreType.DMA(()), pltpu.SemaphoreType.DMA((4,)),
        ],
    )
    came = lax.ppermute(give, "tm", ring)
    far23, near23, edge_a, edge_b = call(
        early_kernel, [sums, sums, edges, edges], fa, w1, flops=10**9, scratch=[pltpu.VMEM((2, 2, COLS, 192), F32)]
    )
    b23 = lax.ppermute(edge_b, ("tm", "rows"), outer)
    a23 = lax.ppermute(edge_a, "rows", inner)
    part = call(between_kernel, [shape((3, 2, 2, COLS, 192), F32)], fa, w1, flops=16 * 10**9)[0]
    near, part_q = call(near_kernel, [half, shape((2, 2, COLS, 192), F32)], a23, near23, b1, g2, w2, flops=10**9)
    far, give = call(
        next_kernel, [half, edges], b23, far23, part_q, b1, g2, w2, flops=10**9,
        scratch=[pltpu.VMEM((2, 2, COLS, 192), F32)],
    )
    q = lax.ppermute(give, "tm", ring)
    frames, far01, mid, edge = call(
        late_kernel, [shape((2, 2, COLS, 1152)), sums, sums, edges], came, part, w1, far, flops=10**9
    )
    b01 = lax.ppermute(edge, ("tm", "rows"), outer)
    near01, edge = call(inner_kernel, [sums, edges], frames, mid, part, w1, flops=10**9)
    a01 = lax.ppermute(edge, "rows", inner)
    rest = call(rest_kernel, [shape((2, 4, COLS, 192), F32)], near, far, w2, x, sw, b2, sb, flops=16*10**9)[0]
    total = call(
        second_near_kernel, [shape((2, 4, COLS, 192), F32)], a01, near01, b1, g2, w2, rest, flops=10**9,
        scratch=[pltpu.VMEM((2, 2, COLS, 576), BF16)],
    )[0]
    return call(
        second_kernel, [shape((4, 2, COLS, 192))], q, b01, far01, total, b1, g2, w2, flops=10**9,
        scratch=[pltpu.VMEM((2, 4, COLS, 192), F32), pltpu.VMEM((2, 2, COLS, 576), BF16)],
    )[0]


def solution(mesh):
    return jax.shard_map(
        per_device,
        mesh=mesh,
        in_specs=(P("tm", "rows", None, None), P(), P(), P(), P(), P(), P(), P(), P()),
        out_specs=P("tm", "rows", None, None),
        check_vma=False,
    )
```

```python
import jax
import jax.numpy as jnp
from jax import lax
from jax.experimental import pallas as pl
from jax.experimental.pallas import tpu as pltpu
from jax.sharding import PartitionSpec as P

F32 = jnp.float32
BF16 = jnp.bfloat16
COLS = 64
VMEM = pl.BlockSpec(memory_space=pltpu.VMEM)
HBM = pl.BlockSpec(memory_space=pltpu.HBM)


def call(body, outs, *args, flops=0, scratch=(), limit=8, in_hbm=()):
    args = [pltpu.with_memory_space_constraint(a, pltpu.HBM) if n in in_hbm else a for n, a in enumerate(args)]
    moved = sum(a.size * a.dtype.itemsize for a in args) + sum(o.size * o.dtype.itemsize for o in outs)
    return pl.pallas_call(
        body,
        out_shape=outs,
        in_specs=[HBM if n in in_hbm else VMEM for n in range(len(args))],
        out_specs=[VMEM] * len(outs),
        scratch_shapes=list(scratch),
        compiler_params=pltpu.CompilerParams(vmem_limit_bytes=limit << 20),
        cost_estimate=pl.CostEstimate(flops=flops // 10, bytes_accessed=moved // 10, transcendentals=0),
    )(*args)


def shape(dims, dtype=BF16):
    return jax.ShapeDtypeStruct(dims, dtype)


def act(values, gain):
    mean = jnp.mean(values * values, axis=-1, keepdims=True)
    scaled = values * lax.rsqrt(mean + 1e-06) * gain
    half = 0.5 * scaled
    return half + half * jnp.tanh(half)


def taps(values):
    frames, _, channels = values.shape
    flat = values.reshape(frames * COLS, channels)
    col = lax.broadcasted_iota(jnp.int32, flat.shape, 0) % COLS
    left = jnp.where(col == 0, 0.0, pltpu.roll(flat, 1, 0))
    right = jnp.where(col == COLS - 1, 0.0, pltpu.roll(flat, frames * COLS - 1, 0))
    return jnp.concatenate([left, flat, right], axis=-1).astype(BF16).reshape(frames, COLS, 3 * channels)


def first_sums(parts, w_ref):
    a = jnp.concatenate([source.reshape(4 * COLS, 1152) for _, source in parts], axis=-1)
    outs = []
    for j in range(3):
        w = jnp.concatenate([w_ref[i, j, k] for i, _ in parts for k in range(3)], axis=-1)
        out = lax.dot_general(a, w, (((1,), (1,)), ((), ())), preferred_element_type=F32)
        outs.append(out.reshape(2, 2, COLS, 192))
    return outs[2][0], outs[2][1] + outs[1][0], outs[1][1] + outs[0][0], outs[0][1]


def edge_rows(acc_ref, outer):
    odd = lax.axis_index("rows") % 2 == 1
    up = jnp.concatenate([acc_ref[0], acc_ref[1]], axis=-1)
    down = jnp.concatenate([acc_ref[2], acc_ref[3]], axis=-1)
    return jnp.where(odd, down if outer else up, up if outer else down).astype(BF16)


def outer_side():
    return lax.axis_index("rows") % 2


def second_act(own_ref, r_ref, bias_ref, gain_ref, side, outer, sa_ref):
    rows = lax.axis_index("rows")
    edge = jnp.logical_or(rows == 0, rows == lax.axis_size("rows") - 1)
    came = r_ref[...].astype(F32)
    if outer:
        came = jnp.where(edge, 0.0, came)
    for n in range(2):
        hidden = own_ref[2 * side + n] + came[..., 192 * n : 192 * n + 192] + bias_ref[...]
        second = act(hidden.astype(BF16).astype(F32), gain_ref[...])
        if outer:
            second = jnp.where(jnp.logical_and(edge, side == n), 0.0, second)
        for k in range(3):
            sa_ref[n, :, :, 256 * k : 256 * k + 192] = taps(second)[..., 192 * k : 192 * k + 192]
            sa_ref[n, :, :, 256 * k + 192 : 256 * k + 256] = jnp.zeros((2, COLS, 64), BF16)


def second_sums(sa_ref, w_ref, side, parts, acc_ref):
    def dot(a, w):
        count = a.shape[0] * a.shape[1]
        out = jnp.dot(a.reshape(count * COLS, 768), w, preferred_element_type=F32)
        return out.reshape(a.shape[0], a.shape[1], COLS, 192)

    for i, source, frames in parts:
        acc_ref[:, frames] += dot(sa_ref[:, source], w_ref[i, 2 * side])
        acc_ref[pl.ds(side, 1), frames] += dot(sa_ref[pl.ds(1 - side, 1), source], w_ref[i, 1])


def act_kernel(x_hbm, g_hbm, fa_ref, t_ref, x_ref, g_ref, gsem, sem):
    gain_load = pltpu.make_async_copy(g_hbm, g_ref, gsem)
    loads = [pltpu.make_async_copy(x_hbm.at[t], x_ref.at[t], sem.at[t]) for t in range(4)]
    for load in [gain_load] + loads:
        load.start()
    gain_load.wait()
    gain = g_ref[...].reshape(1, 384)
    for t in range(4):
        loads[t].wait()
        for row in range(2):
            value = act(x_ref[t, row].astype(F32), gain)
            fa_ref[row, t] = taps(value[None])[0]
            if t >= 2:
                t_ref[row, t - 2] = value.astype(BF16)


def early_kernel(fa_ref, w_ref, own_ref, a_ref, b_ref):
    for row, total in enumerate(first_sums([(i, fa_ref[:, i : i + 2]) for i in range(3)], w_ref)):
        own_ref[row] = total
    a_ref[...] = edge_rows(own_ref, False)
    b_ref[...] = edge_rows(own_ref, True)


def between_kernel(fa_ref, w_ref, part_ref):
    first = fa_ref[:, 0:1]
    parts = [(2, fa_ref[:, 0:2]), (1, jnp.concatenate([jnp.zeros_like(first), first], axis=1))]
    for row, total in enumerate(first_sums(parts, w_ref)):
        part_ref[row] = total


def late_kernel(t_ref, part_ref, w_ref, after_ref, own_ref, a_ref, b_ref, fa_ref):
    del after_ref
    first = lax.axis_index("tm") == 0
    for row in range(2):
        fa_ref[row] = taps(jnp.where(first, 0.0, t_ref[row].astype(F32)))
    last = fa_ref[:, 1:2]
    parts = [(0, fa_ref[...]), (1, jnp.concatenate([last, jnp.zeros_like(last)], axis=1))]
    for row, total in enumerate(first_sums(parts, w_ref)):
        own_ref[row] = part_ref[row] + total
    a_ref[...] = edge_rows(own_ref, False)
    b_ref[...] = edge_rows(own_ref, True)


NEXT = [(0, slice(0, 2), slice(0, 2)), (1, slice(1, 2), slice(0, 1))]
REST = [(2, slice(0, 2), slice(2, 4)), (1, slice(0, 1), slice(3, 4))]
FIRST = [(i, slice(0, 2), slice(2 - i, 4 - i)) for i in range(3)]


def widen_kernel(w_ref, wide_ref):
    for i in range(3):
        for j in range(3):
            for k in range(3):
                wide_ref[i, j, 256 * k : 256 * k + 192] = w_ref[i, j, k]
                wide_ref[i, j, 256 * k + 192 : 256 * k + 256] = jnp.zeros((64, 192), BF16)


def near_kernel(ra_ref, own_ref, bias_ref, gain_ref, w_ref, sa_ref, q_ref):
    side = 1 - outer_side()
    second_act(own_ref, ra_ref, bias_ref, gain_ref, side, False, sa_ref)
    q_ref[...] = jnp.zeros_like(q_ref)
    second_sums(sa_ref, w_ref, side, NEXT, q_ref)


def next_kernel(rb_ref, own_ref, part_ref, bias_ref, gain_ref, w_ref, sa_ref, q_ref, acc_ref):
    side = outer_side()
    second_act(own_ref, rb_ref, bias_ref, gain_ref, side, True, sa_ref)
    acc_ref[...] = part_ref[...]
    second_sums(sa_ref, w_ref, side, NEXT, acc_ref)
    q_ref[...] = jnp.concatenate([acc_ref[0], acc_ref[1]], axis=-1).astype(BF16)


def rest_kernel(near_ref, far_ref, w_ref, x_ref, sw_ref, bias_ref, sbias_ref, acc_ref):
    bias = bias_ref[...] + sbias_ref[...]
    for row in range(2):
        skip = lax.dot_general(
            x_ref[:, row].reshape(4 * COLS, 384), sw_ref[...], (((1,), (1,)), ((), ())), preferred_element_type=F32
        )
        acc_ref[row] = skip.reshape(4, COLS, 192) + bias
    second_sums(near_ref, w_ref, 1 - outer_side(), REST, acc_ref)
    second_sums(far_ref, w_ref, outer_side(), REST, acc_ref)


def second_near_kernel(ra_ref, own_ref, bias_ref, gain_ref, w_ref, rest_ref, acc_ref, sa_ref):
    side = 1 - outer_side()
    second_act(own_ref, ra_ref, bias_ref, gain_ref, side, False, sa_ref)
    acc_ref[...] = rest_ref[...]
    second_sums(sa_ref, w_ref, side, FIRST, acc_ref)


def second_kernel(q_ref, rb_ref, own_ref, part_ref, bias_ref, gain_ref, w_ref, out_ref, acc_ref, sa_ref):
    side = outer_side()
    second_act(own_ref, rb_ref, bias_ref, gain_ref, side, True, sa_ref)
    acc_ref[...] = part_ref[...]
    second_sums(sa_ref, w_ref, side, FIRST, acc_ref)
    came = jnp.where(lax.axis_index("tm") == 0, 0.0, q_ref[...].astype(F32))
    for row in range(2):
        out_ref[0:2, row] = (acc_ref[row, 0:2] + came[..., 192 * row : 192 * row + 192]).astype(BF16)
        out_ref[2:4, row] = acc_ref[row, 2:4].astype(BF16)


def swap_pairs(steps, count):
    inner = [(i, i ^ 1) for i in range(count)]
    outer = []
    for t in range(steps):
        base = t * count
        for i in range(1, count - 1, 2):
            outer += [(base + i, base + i + 1), (base + i + 1, base + i)]
        for i in (0, count - 1):
            outer.append((base + i, (t ^ 1) * count + i))
    return inner, outer


def per_device(x, w1, b1, g1, w2, b2, g2, sw, sb):
    steps = lax.axis_size("tm")
    inner, outer = swap_pairs(steps, lax.axis_size("rows"))
    ring = [(i, (i + 1) % steps) for i in range(steps)]
    w1 = jnp.swapaxes(w1, 3, 4)
    sw = jnp.swapaxes(sw, 0, 1)
    b1, b2, g2, sb = (v.reshape(1, -1) for v in (b1, b2, g2, sb))
    half = shape((2, 2, COLS, 768))
    sums, edges = shape((4, 2, COLS, 192), F32), shape((2, COLS, 384))

    fa, give = call(
        act_kernel, [shape((2, 4, COLS, 1152)), shape((2, 2, COLS, 384))], x, g1, flops=4 * 10**10, in_hbm=(0, 1),
        scratch=[
            pltpu.VMEM((4, 2, COLS, 384), BF16), pltpu.VMEM((384,), F32),
            pltpu.SemaphoreType.DMA(()), pltpu.SemaphoreType.DMA((4,)),
        ],
    )
    came = lax.ppermute(give, "tm", ring)
    own23, edge_a, edge_b = call(early_kernel, [sums, edges, edges], fa, w1, flops=10**9)
    b23 = lax.ppermute(edge_b, ("tm", "rows"), outer)
    a23 = lax.ppermute(edge_a, "rows", inner)
    part = call(between_kernel, [sums], fa, w1, flops=16*10**9)[0]
    w2 = call(widen_kernel, [shape((3, 3, 768, 192))], w2)[0]
    near, part_q = call(near_kernel, [half, shape((2, 2, COLS, 192), F32)], a23, own23, b1, g2, w2, flops=10**9)
    far, give = call(
        next_kernel, [half, edges], b23, own23, part_q, b1, g2, w2, flops=10**9,
        scratch=[pltpu.VMEM((2, 2, COLS, 192), F32)],
    )
    q = lax.ppermute(give, "tm", ring)
    own01, edge_a, edge_b = call(
        late_kernel, [sums, edges, edges], came, part, w1, far, flops=10**9,
        scratch=[pltpu.VMEM((2, 2, COLS, 1152), BF16)],
    )
    b01 = lax.ppermute(edge_b, ("tm", "rows"), outer)
    a01 = lax.ppermute(edge_a, "rows", inner)
    rest = call(rest_kernel, [shape((2, 4, COLS, 192), F32)], near, far, w2, x, sw, b2, sb, flops=16*10**9)[0]
    total = call(
        second_near_kernel, [shape((2, 4, COLS, 192), F32)], a01, own01, b1, g2, w2, rest, flops=10**9,
        scratch=[pltpu.VMEM((2, 2, COLS, 768), BF16)],
    )[0]
    return call(
        second_kernel, [shape((4, 2, COLS, 192))], q, b01, own01, total, b1, g2, w2, flops=10**9,
        scratch=[pltpu.VMEM((2, 4, COLS, 192), F32), pltpu.VMEM((2, 2, COLS, 768), BF16)],
    )[0]


def solution(mesh):
    return jax.shard_map(
        per_device,
        mesh=mesh,
        in_specs=(P("tm", "rows", None, None), P(), P(), P(), P(), P(), P(), P(), P()),
        out_specs=P("tm", "rows", None, None),
        check_vma=False,
    )
```
